512 devices in a mesh: view: 8 (over y_lo, core), pencil: 64 (over y_hi, z, x).
Axes of the slice: x: 4, y: 8 (y_hi: 2, y_lo: 4; y = y_hi * 4 + y_lo), z: 8, core: 2. Of those that a mesh axis runs over, the one named last changes fastest.
Arguments:
- estimate: float32 [512, 16, 512], P('pencil'), may hold values from 0.5 to 2
- views_data: float32 [8, 512, 16, 512], P('view', 'pencil'), may hold values from 0.5 to 2
- psf_long: float32 [8, 61], P('view'), may hold values from 0.05 to 1
- psf_short: float32 [8, 2, 15], P('view'), may hold values from 0.05 to 1
- detection: int32 [8, 2], P('view'), may hold values from -12 to 12, as said below
Outputs:
- updated: float32 [512, 16, 512], P('pencil')
The draws below stay inside these ranges and needn't reach their ends.
Inputs may be any that keep to these rules, and one draw needn't show every extreme that they name: `detection`: column 0 is 0 or 1; column 1 lies between -12 and 12, and some view has offset 12 and another -12.
All inputs are finite; a program needn't handle non-finite values.
Results may differ from the reference program's by a relative error of at most 0.0003.
Values sent between devices are 32-bit elements; how exact they have to be, the bound alone decides.
A program may use at most 64 MiB of HBM per device.

```python
import math
import jax
import jax.numpy as jnp
from jax import lax

X = 512
Y = 16
Z = 512
LONG_TAPS = 61
SHORT_TAPS = 15
VIEWS = 8


def draw_detection(key, part):
    axis_key = jax.random.fold_in(key, 11)
    shift_key = jax.random.fold_in(key, 23)
    order_key = jax.random.fold_in(key, 37)
    axis_bits = jax.random.randint(axis_key, (VIEWS,), 0, 2, dtype=jnp.int32)
    shifts = jax.random.randint(shift_key, (VIEWS,), -12, 13, dtype=jnp.int32)
    order = jax.random.permutation(order_key, VIEWS)
    shifts = shifts.at[order[0]].set(jnp.int32(12))
    shifts = shifts.at[order[1]].set(jnp.int32(-12))
    return jnp.stack([axis_bits, shifts], axis=1)


def steps_of(key, extent, pieces, least, largest):
    gain, own = 1.0, jax.random.fold_in(key, 6)
    for dim, shards_of in pieces:
        steps = jnp.exp(jax.random.uniform(jax.random.fold_in(own, dim), (shards_of,), jnp.float32, least / len(pieces), largest / len(pieces)))
        gain = gain * jnp.repeat(steps, extent[dim] // shards_of).reshape([-1 if axis == dim else 1 for axis in range(len(extent))])
    return gain


def setup_inputs(seed: int = 0) -> dict:
    splits = jax.random.split(jax.random.key(seed), 6)
    estimate = jnp.clip(jnp.exp(math.log(2.0) - 1.3862944 * jax.random.uniform(splits[0], (X, Y, Z), jnp.float32) ** steps_of(splits[0], (X, Y, Z), ((0, 64),), -0.2, 0.2)), 0.5, 2.0)
    views_data = jnp.clip(jnp.exp(math.log(2.0) - 1.3862944 * jax.random.uniform(splits[1], (VIEWS, Z, Y, X), jnp.float32) ** steps_of(splits[1], (VIEWS, Z, Y, X), ((0, 8), (1, 64)), -0.2, 0.2)), 0.5, 2.0)
    psf_long = jnp.clip(jnp.exp(math.log(1.0) - 2.9957323 * jax.random.uniform(splits[2], (VIEWS, LONG_TAPS), jnp.float32) ** steps_of(splits[2], (VIEWS, LONG_TAPS), ((0, 8),), -0.2, 0.2)), 0.05, 1.0)
    psf_short = jnp.clip(jnp.exp(math.log(1.0) - 2.9957323 * jax.random.uniform(splits[3], (VIEWS, 2, SHORT_TAPS), jnp.float32) ** steps_of(splits[3], (VIEWS, 2, SHORT_TAPS), ((0, 8),), -0.2, 0.2)), 0.05, 1.0)
    detection = draw_detection(jax.random.fold_in(splits[5], 71), 0)
    return dict(estimate=estimate, views_data=views_data, psf_long=psf_long, psf_short=psf_short, detection=detection)


def banded(taps, length, shift):
    count = taps.shape[0]
    radius = (count - 1) // 2
    rows = jnp.arange(length, dtype=jnp.int32)[:, None]
    cols = jnp.arange(length, dtype=jnp.int32)[None, :]
    offset = cols - rows + radius - shift.astype(jnp.int32)
    valid = (offset >= 0) & (offset < count)
    return jnp.where(valid, jnp.take(taps, jnp.clip(offset, 0, count - 1)), jnp.zeros((), taps.dtype))


def view_taps(long_raw, short_raw, detect):
    long_taps = long_raw / jnp.sum(long_raw)
    short_taps = short_raw / jnp.sum(short_raw, axis=-1, keepdims=True)
    margin = (long_taps.shape[0] - short_taps.shape[1]) // 2
    padded = jnp.pad(short_taps, ((0, 0), (margin, margin)))
    axis_bit = detect[0]
    first = jnp.where(axis_bit == 0, long_taps, padded[0])
    third = jnp.where(axis_bit == 0, padded[0], long_taps)
    zero = jnp.zeros((), jnp.int32)
    first_shift = jnp.where(axis_bit == 0, detect[1], zero).astype(jnp.int32)
    third_shift = jnp.where(axis_bit == 0, zero, detect[1]).astype(jnp.int32)
    return first, padded[1], third, first_shift, third_shift


def one_view(estimate, record, long_raw, short_raw, detect):
    high = lax.Precision.HIGHEST
    first, second, third, first_shift, third_shift = view_taps(long_raw, short_raw, detect)
    x_matrix = banded(first, estimate.shape[0], first_shift)
    y_matrix = banded(second, estimate.shape[1], jnp.zeros((), jnp.int32))
    z_matrix = banded(third, estimate.shape[2], third_shift)
    field = jnp.einsum('abj,ij->abi', estimate, z_matrix, precision=high)
    field = jnp.einsum('ajc,ij->aic', field, y_matrix, precision=high)
    blurred = jnp.einsum('jbc,ij->cbi', field, x_matrix, precision=high)
    ratio = record / blurred
    back = jnp.einsum('abj,ji->abi', ratio, x_matrix, precision=high)
    back = jnp.einsum('jbc,ji->cbi', back, z_matrix, precision=high)
    return jnp.einsum('ajc,ji->aic', back, y_matrix, precision=high)


def reference(estimate, views_data, psf_long, psf_short, detection):
    def step(factor, inputs):
        record, long_raw, short_raw, detect = inputs
        return factor * one_view(estimate, record, long_raw, short_raw, detect), None

    factor, _ = lax.scan(step, jnp.ones(estimate.shape, jnp.float32), (views_data, psf_long, psf_short, detection))
    return estimate * factor
```

```python
import functools

import jax
import jax.numpy as jnp
from jax import lax
from jax.experimental import pallas as pl
from jax.experimental.pallas import tpu as pltpu
from jax.sharding import PartitionSpec as P

F32 = jnp.float32
BF16 = jnp.bfloat16
MESH = pl.DeviceIdType.MESH

VIEWS = 8
PENCILS = 64
TILE = 8
N = 512
L = 128
YDIM = 16

NN = (((1,), (0,)), ((), ()))
NT = (((1,), (1,)), ((), ()))

OFFSETS = sorted(
    ((a, b, c) for a in range(2) for b in range(8) for c in range(4) if a + b + c),
    key=lambda o: (-(4 * o[0] + min(o[1], 8 - o[1]) + min(o[2], 4 - o[2])), o),
)


def split(a):
    hi = a.astype(BF16)
    lo = (a - hi.astype(F32)).astype(BF16)
    return hi, lo


def dot3(a, b, dims):
    ah, al = a
    bh, bl = b
    dot = functools.partial(
        lax.dot_general, dimension_numbers=dims, preferred_element_type=F32
    )
    return dot(ah, bh) + (dot(ah, bl) + dot(al, bh))


def roll(x, shift, axis):
    return pltpu.roll(x, shift % x.shape[axis], axis)


def shifted(row, amount):
    for bit in range(5):
        flag = ((amount >> bit) & 1) == 1
        row = jnp.where(flag, roll(row, 1 << bit, 1), row)
    return row


def staircase(row, start):
    eight = jnp.broadcast_to(row, (8, row.shape[1]))
    eight = pltpu.roll(eight, 0, 1, stride=1, stride_axis=0)
    return jnp.concatenate([roll(eight, start + 8 * k, 1) for k in range(L // 8)], axis=0)


def band_blocks(row, amount):
    row = shifted(row, amount + 12)
    wide = jnp.concatenate([row, jnp.zeros((1, 2 * L), F32)], axis=1)
    return staircase(wide, 86)


def y_block(row):
    full = staircase(row, 121)
    rows = lax.broadcasted_iota(jnp.int32, (L, L), 0) // YDIM
    cols = lax.broadcasted_iota(jnp.int32, (L, L), 1) // YDIM
    return jnp.where(rows == cols, full, 0.0)


def swap_slab(x):
    x = x.reshape(PENCILS, TILE, L)
    sub = lax.broadcasted_iota(jnp.int32, x.shape, 1)
    lane = lax.broadcasted_iota(jnp.int32, x.shape, 2) // YDIM
    for bit in (4, 2, 1):
        s_bit = (sub // bit) % 2
        same = s_bit == (lane // bit) % 2
        up = roll(roll(x, -bit, 1), YDIM * bit, 2)
        down = up if bit == 4 else roll(roll(x, bit, 1), -YDIM * bit, 2)
        x = jnp.where(same, x, jnp.where(s_bit == 0, up, down))
    return x.reshape(PENCILS * TILE, L)


def taps(long_ref, short_ref, detect_ref, rows):
    rows[...] = jnp.zeros_like(rows)
    rows[0:1, 0 : long_ref.shape[1]] = long_ref[...]
    rows[1:3, 0 : short_ref.shape[2]] = short_ref[0]
    value = rows[...]
    value = value / jnp.maximum(jnp.sum(value, axis=1, keepdims=True), 1e-30)
    along, across, second = value[0:1], roll(value[1:2], 23, 1), value[2:3]
    is_first = detect_ref[0, 0] == 0
    offset = detect_ref[0, 1]
    first = jnp.where(is_first, along, across)
    third = jnp.where(is_first, across, along)
    return (
        (first, jnp.where(is_first, offset, 0)),
        second,
        (third, jnp.where(is_first, 0, offset)),
    )


def store_pair(ref, rows, cols, value):
    hi, lo = split(value)
    ref[0, rows, cols] = hi
    ref[1, rows, cols] = lo


def fill_rows(ref, blocks):
    zero = jnp.zeros((L, L), BF16)
    for part in range(2):
        ref[part, 0:L, 3 * L : 4 * L] = zero
        ref[part, L : 2 * L, 0:L] = zero
    store_pair(ref, slice(0, L), slice(0, 3 * L), blocks)
    store_pair(ref, slice(L, 2 * L), slice(L, 4 * L), blocks)


def fill_cols(ref, blocks):
    zero = jnp.zeros((L, L), BF16)
    left, here, right = (blocks[:, k * L : (k + 1) * L] for k in range(3))
    for part in range(2):
        ref[part, 0:L, L : 2 * L] = zero
        ref[part, 3 * L : 4 * L, 0:L] = zero
    for col in range(2):
        for row, value in enumerate((right, here, left)):
            store_pair(
                ref,
                slice((row + col) * L, (row + col + 1) * L),
                slice(col * L, (col + 1) * L),
                value,
            )


HALVES = ((0, slice(L, 4 * L), slice(0, 3 * L)), (1, slice(0, 3 * L), slice(L, 4 * L)))


def kernel(
    est_ref, views_ref, long_ref, short_ref, detect_ref, out_ref,
    rows, zrow, zcol, xrow, xtrow, ymat, views_t,
    send1, recv1, send2, recv2, corr, gathered,
    ssem, rsem,
):
    v = lax.axis_index("view")
    q = lax.axis_index("pencil")
    x, z, yh = q % 4, (q // 4) % 8, q // 32

    def pencil(off):
        a, b, c = off
        return (((yh + a) % 2) * 8 + (z + b) % 8) * 4 + (x + c) % 4

    barrier = pltpu.get_barrier_semaphore()
    for off in OFFSETS:
        pl.semaphore_signal(barrier, inc=1, device_id=(v, pencil(off)), device_id_type=MESH)
    for k in range(1, VIEWS):
        pl.semaphore_signal(barrier, inc=1, device_id=((v + k) % VIEWS, q), device_id_type=MESH)

    (first, first_shift), second, (third, third_shift) = taps(
        long_ref, short_ref, detect_ref, rows
    )
    yb = y_block(second)
    store_pair(ymat, slice(0, L), slice(0, L), yb)
    zb = band_blocks(third, third_shift)
    fill_rows(zrow, zb)

    est = est_ref[...]
    field = dot3(split(yb), split(est), NN)
    fh, fl = split(field)
    for half, cols, window in HALVES:
        send1[half * 256 : (half + 1) * 256, :] = dot3(
            (zrow[0, :, cols], zrow[1, :, cols]), (fh[:, window], fl[:, window]), NT
        )

    pl.semaphore_wait(barrier, PENCILS - 1 + VIEWS - 1)

    def exchange(src, dst, k):
        mine = pl.ds(pl.multiple_of(q * TILE, TILE), TILE)
        for off in OFFSETS:
            peer = pencil(off)
            pltpu.make_async_remote_copy(
                src_ref=src.at[pl.ds(pl.multiple_of(peer * TILE, TILE), TILE), :],
                dst_ref=dst.at[mine, :],
                send_sem=ssem.at[k],
                recv_sem=rsem.at[k],
                device_id=(v, peer),
                device_id_type=MESH,
            ).start()
        dst[mine, :] = src[mine, :]

    def arrived(src, dst, k, count):
        span = pl.ds(0, count)
        both = pltpu.make_async_copy(src.at[span], dst.at[span], rsem.at[k])
        both.wait()
        pltpu.make_async_copy(src.at[span], dst.at[span], ssem.at[k]).wait()

    exchange(send1, recv1, 0)
    xb = band_blocks(first, first_shift)
    fill_rows(xrow, xb)
    fill_rows(
        xtrow,
        jnp.concatenate([xb[:, k * L : (k + 1) * L].T for k in (2, 1, 0)], axis=1),
    )
    fill_cols(zcol, zb)
    ytb = split(yb.T)
    views_t[...] = views_ref[...].T
    arrived(send1, recv1, 0, (PENCILS - 1) * TILE)

    gh, gl = split(swap_slab(recv1[...]))
    ratio = []
    for half, cols, window in HALVES:
        blurred = dot3(
            (xrow[0, :, cols], xrow[1, :, cols]), (gh[window], gl[window]), NN
        )
        ratio.append(views_t[half * 256 : (half + 1) * 256, :] / blurred)
    rh, rl = split(jnp.concatenate(ratio, axis=0))
    back = jnp.concatenate(
        [
            dot3((xtrow[0, :, cols], xtrow[1, :, cols]), (rh[window], rl[window]), NN)
            for _, cols, window in HALVES
        ],
        axis=0,
    )
    send2[...] = swap_slab(back)
    exchange(send2, recv2, 1)
    arrived(send2, recv2, 1, (PENCILS - 1) * TILE)

    bh, bl = split(recv2[...].T)
    whole = jnp.concatenate(
        [
            dot3((bh[:, window], bl[:, window]), (zcol[0, rows_, :], zcol[1, rows_, :]), NN)
            for _, rows_, window in HALVES
        ],
        axis=1,
    )
    corr[...] = dot3(ytb, split(whole), NN)

    slab = pl.ds(pl.multiple_of(v * YDIM, YDIM), YDIM)
    for k in range(1, VIEWS):
        peer = (v + k) % VIEWS
        pltpu.make_async_remote_copy(
            src_ref=corr.at[pl.ds(pl.multiple_of(peer * YDIM, YDIM), YDIM), :],
            dst_ref=gathered.at[slab, :],
            send_sem=ssem.at[2],
            recv_sem=rsem.at[2],
            device_id=(peer, q),
            device_id_type=MESH,
        ).start()
    gathered[slab, :] = corr[slab, :]
    arrived(corr, gathered, 2, (VIEWS - 1) * YDIM)
    factor = gathered[0:YDIM, :]
    for k in range(1, VIEWS):
        factor = factor * gathered[k * YDIM : (k + 1) * YDIM, :]
    out_ref[slab, :] = est_ref[slab, :] * factor
    for k in range(1, VIEWS):
        pltpu.make_async_remote_copy(
            src_ref=out_ref.at[slab, :],
            dst_ref=out_ref.at[slab, :],
            send_sem=ssem.at[3],
            recv_sem=rsem.at[3],
            device_id=((v + k) % VIEWS, q),
            device_id_type=MESH,
        ).start()
    arrived(out_ref, out_ref, 3, (VIEWS - 1) * YDIM)


def per_device(estimate, views_data, psf_long, psf_short, detection):
    vmem = pl.BlockSpec(memory_space=pltpu.VMEM)
    flat = pl.pallas_call(
        kernel,
        out_shape=jax.ShapeDtypeStruct((L, N), F32),
        in_specs=[vmem, vmem, vmem, vmem, pl.BlockSpec(memory_space=pltpu.SMEM)],
        out_specs=vmem,
        scratch_shapes=[
            pltpu.VMEM((8, L), F32),
            pltpu.VMEM((2, 2 * L, 4 * L), BF16),
            pltpu.VMEM((2, 4 * L, 2 * L), BF16),
            pltpu.VMEM((2, 2 * L, 4 * L), BF16),
            pltpu.VMEM((2, 2 * L, 4 * L), BF16),
            pltpu.VMEM((2, L, L), BF16),
            pltpu.VMEM((N, L), F32),
            pltpu.VMEM((N, L), F32),
            pltpu.VMEM((N, L), F32),
            pltpu.VMEM((N, L), F32),
            pltpu.VMEM((N, L), F32),
            pltpu.VMEM((L, N), F32),
            pltpu.VMEM((L, N), F32),
            pltpu.SemaphoreType.DMA((4,)),
            pltpu.SemaphoreType.DMA((4,)),
        ],
        compiler_params=pltpu.CompilerParams(collective_id=0, has_side_effects=True),
    )(
        estimate.reshape(L, N),
        views_data.reshape(L, N),
        psf_long,
        psf_short,
        detection,
    )
    return flat.reshape(estimate.shape)


def solution(mesh):
    return jax.shard_map(
        per_device,
        mesh=mesh,
        in_specs=(
            P("pencil", None, None),
            P("view", "pencil", None, None),
            P("view", None),
            P("view", None, None),
            P("view", None),
        ),
        out_specs=P("pencil", None, None),
        check_vma=False,
    )
```

```python
import functools

import jax
import jax.numpy as jnp
from jax import lax
from jax.experimental import pallas as pl
from jax.experimental.pallas import tpu as pltpu
from jax.sharding import PartitionSpec as P

F32 = jnp.float32
BF16 = jnp.bfloat16
MESH = pl.DeviceIdType.MESH

VIEWS = 8
CHIPS = 4
PENCILS = 64
TILE = 8
N = 512
L = 128
YDIM = 16

NN = (((1,), (0,)), ((), ()))
NT = (((1,), (1,)), ((), ()))

OFFSETS = sorted(
    ((a, b, c) for a in range(2) for b in range(8) for c in range(4) if a + b + c),
    key=lambda o: (-(4 * o[0] + min(o[1], 8 - o[1]) + min(o[2], 4 - o[2])), o),
)


def split(a):
    hi = a.astype(BF16)
    lo = (a - hi.astype(F32)).astype(BF16)
    return hi, lo


def dot3(a, b, dims):
    ah, al = a
    bh, bl = b
    dot = functools.partial(
        lax.dot_general, dimension_numbers=dims, preferred_element_type=F32
    )
    return dot(ah, bh) + (dot(ah, bl) + dot(al, bh))


def roll(x, shift, axis):
    return pltpu.roll(x, shift % x.shape[axis], axis)


def shifted(row, amount):
    for bit in range(5):
        flag = ((amount >> bit) & 1) == 1
        row = jnp.where(flag, roll(row, 1 << bit, 1), row)
    return row


def staircase(row, start):
    eight = jnp.broadcast_to(row, (8, row.shape[1]))
    eight = pltpu.roll(eight, 0, 1, stride=1, stride_axis=0)
    return jnp.concatenate([roll(eight, start + 8 * k, 1) for k in range(L // 8)], axis=0)


def band_blocks(row, amount):
    row = shifted(row, amount + 12)
    wide = jnp.concatenate([row, jnp.zeros((1, 2 * L), F32)], axis=1)
    return staircase(wide, 86)


def y_block(row):
    full = staircase(row, 121)
    rows = lax.broadcasted_iota(jnp.int32, (L, L), 0) // YDIM
    cols = lax.broadcasted_iota(jnp.int32, (L, L), 1) // YDIM
    return jnp.where(rows == cols, full, 0.0)


def swap_slab(x):
    x = x.reshape(PENCILS, TILE, L)
    sub = lax.broadcasted_iota(jnp.int32, x.shape, 1)
    lane = lax.broadcasted_iota(jnp.int32, x.shape, 2) // YDIM
    for bit in (4, 2, 1):
        s_bit = (sub // bit) % 2
        same = s_bit == (lane // bit) % 2
        up = roll(roll(x, -bit, 1), YDIM * bit, 2)
        down = up if bit == 4 else roll(roll(x, bit, 1), -YDIM * bit, 2)
        x = jnp.where(same, x, jnp.where(s_bit == 0, up, down))
    return x.reshape(PENCILS * TILE, L)


def taps(long_ref, short_ref, detect_ref, rows):
    rows[...] = jnp.zeros_like(rows)
    rows[0:1, 0 : long_ref.shape[1]] = long_ref[...]
    rows[1:3, 0 : short_ref.shape[2]] = short_ref[0]
    value = rows[...]
    value = value / jnp.maximum(jnp.sum(value, axis=1, keepdims=True), 1e-30)
    along, across, second = value[0:1], roll(value[1:2], 23, 1), value[2:3]
    is_first = detect_ref[0, 0] == 0
    offset = detect_ref[0, 1]
    first = jnp.where(is_first, along, across)
    third = jnp.where(is_first, across, along)
    return (
        (first, jnp.where(is_first, offset, 0)),
        second,
        (third, jnp.where(is_first, 0, offset)),
    )


def store_pair(ref, rows, cols, value):
    hi, lo = split(value)
    ref[0, rows, cols] = hi
    ref[1, rows, cols] = lo


def fill_rows(ref, blocks):
    zero = jnp.zeros((L, L), BF16)
    for part in range(2):
        ref[part, 0:L, 3 * L : 4 * L] = zero
        ref[part, L : 2 * L, 0:L] = zero
    store_pair(ref, slice(0, L), slice(0, 3 * L), blocks)
    store_pair(ref, slice(L, 2 * L), slice(L, 4 * L), blocks)


def fill_cols(ref, blocks):
    zero = jnp.zeros((L, L), BF16)
    left, here, right = (blocks[:, k * L : (k + 1) * L] for k in range(3))
    for part in range(2):
        ref[part, 0:L, L : 2 * L] = zero
        ref[part, 3 * L : 4 * L, 0:L] = zero
    for col in range(2):
        for row, value in enumerate((right, here, left)):
            store_pair(
                ref,
                slice((row + col) * L, (row + col + 1) * L),
                slice(col * L, (col + 1) * L),
                value,
            )


HALVES = ((0, slice(L, 4 * L), slice(0, 3 * L)), (1, slice(0, 3 * L), slice(L, 4 * L)))


def kernel(
    est_hbm, views_hbm, long_hbm, short_hbm, detect_hbm, out_ref,
    est_ref, views_ref, long_ref, short_ref, detect_ref,
    rows, zrow, zcol, xrow, xtrow, views_t,
    send1, recv1, send2, recv2, corr, pair, part, merged,
    isem, ssem, rsem, pair_ssem, pair_rsem, part_ssem, part_rsem,
    chip_ssem, chip_rsem, core_ssem, core_rsem,
):
    v = lax.axis_index("view")
    q = lax.axis_index("pencil")
    x, z, yh = q % 4, (q // 4) % 8, q // 32

    def pencil(off):
        a, b, c = off
        return (((yh + a) % 2) * 8 + (z + b) % 8) * 4 + (x + c) % 4

    barrier = pltpu.get_barrier_semaphore()
    for off in OFFSETS:
        pl.semaphore_signal(barrier, inc=1, device_id=(v, pencil(off)), device_id_type=MESH)
    core, chip = v % 2, v // 2
    partner = (chip * 2 + (1 - core), q)
    chips = [(3 - chip) % CHIPS, (chip + 2) % CHIPS, (5 - chip) % CHIPS]
    pl.semaphore_signal(barrier, inc=1, device_id=partner, device_id_type=MESH)
    for other in chips:
        pl.semaphore_signal(
            barrier, inc=1, device_id=(other * 2 + core, q), device_id_type=MESH
        )

    loads = [
        pltpu.make_async_copy(src, dst, isem.at[k])
        for k, (src, dst) in enumerate(
            (
                (long_hbm, long_ref),
                (short_hbm, short_ref),
                (detect_hbm, detect_ref),
                (est_hbm, est_ref),
                (views_hbm, views_ref),
            )
        )
    ]
    for load in loads:
        load.start()
    for load in loads[:3]:
        load.wait()

    (first, first_shift), second, (third, third_shift) = taps(
        long_ref, short_ref, detect_ref, rows
    )
    yb = y_block(second)
    zb = band_blocks(third, third_shift)
    fill_rows(zrow, zb)

    loads[3].wait()
    field = dot3(split(yb), split(est_ref[...]), NN)
    fh, fl = split(field)
    for half, cols, window in HALVES:
        send1[half * 256 : (half + 1) * 256, :] = dot3(
            (zrow[0, :, cols], zrow[1, :, cols]), (fh[:, window], fl[:, window]), NT
        )

    pl.semaphore_wait(barrier, PENCILS - 1 + CHIPS)

    def exchange(src, dst, k):
        mine = pl.ds(pl.multiple_of(q * TILE, TILE), TILE)
        for off in OFFSETS:
            peer = pencil(off)
            pltpu.make_async_remote_copy(
                src_ref=src.at[pl.ds(pl.multiple_of(peer * TILE, TILE), TILE), :],
                dst_ref=dst.at[mine, :],
                send_sem=ssem.at[k],
                recv_sem=rsem.at[k],
                device_id=(v, peer),
                device_id_type=MESH,
            ).start()
        dst[mine, :] = src[mine, :]

    def arrived(src, dst, k, count):
        span = pl.ds(0, count)
        both = pltpu.make_async_copy(src.at[span], dst.at[span], rsem.at[k])
        both.wait()
        pltpu.make_async_copy(src.at[span], dst.at[span], ssem.at[k]).wait()

    exchange(send1, recv1, 0)
    xb = band_blocks(first, first_shift)
    fill_rows(xrow, xb)
    fill_rows(
        xtrow,
        jnp.concatenate([xb[:, k * L : (k + 1) * L].T for k in (2, 1, 0)], axis=1),
    )
    fill_cols(zcol, zb)
    ytb = split(yb.T)
    loads[4].wait()
    views_t[...] = views_ref[...].T
    arrived(send1, recv1, 0, (PENCILS - 1) * TILE)

    gh, gl = split(swap_slab(recv1[...]))
    ratio = []
    for half, cols, window in HALVES:
        blurred = dot3(
            (xrow[0, :, cols], xrow[1, :, cols]), (gh[window], gl[window]), NN
        )
        ratio.append(views_t[half * 256 : (half + 1) * 256, :] / blurred)
    rh, rl = split(jnp.concatenate(ratio, axis=0))
    back = jnp.concatenate(
        [
            dot3((xtrow[0, :, cols], xtrow[1, :, cols]), (rh[window], rl[window]), NN)
            for _, cols, window in HALVES
        ],
        axis=0,
    )
    send2[...] = swap_slab(back)
    exchange(send2, recv2, 1)
    arrived(send2, recv2, 1, (PENCILS - 1) * TILE)

    bh, bl = split(recv2[...].T)
    whole = jnp.concatenate(
        [
            dot3((bh[:, window], bl[:, window]), (zcol[0, rows_, :], zcol[1, rows_, :]), NN)
            for _, rows_, window in HALVES
        ],
        axis=1,
    )
    corr[...] = dot3(ytb, split(whole), NN)

    def quarter(c, b):
        return pl.ds(pl.multiple_of((c * CHIPS + b) * YDIM, YDIM), YDIM)

    halves = []
    for k, b in enumerate(chips + [chip]):
        send = pltpu.make_async_remote_copy(
            src_ref=corr.at[quarter(1 - core, b), :],
            dst_ref=pair.at[b],
            send_sem=pair_ssem.at[k],
            recv_sem=pair_rsem.at[k],
            device_id=partner,
            device_id_type=MESH,
        )
        send.start()
        halves.append(send)
    quarters = []
    for k, b in enumerate(chips + [chip]):
        halves[k].wait_recv()
        pair[b] = pair[b] * corr[quarter(core, b), :]
        if k < CHIPS - 1:
            send = pltpu.make_async_remote_copy(
                src_ref=pair.at[b],
                dst_ref=part.at[k],
                send_sem=part_ssem.at[k],
                recv_sem=part_rsem.at[k],
                device_id=(b * 2 + core, q),
                device_id_type=MESH,
            )
            send.start()
            quarters.append(send)
    factor = pair[chip]
    for k, send in enumerate(quarters):
        send.wait_recv()
    for k in range(CHIPS - 1):
        factor = factor * part[k]
    mine = quarter(core, chip)
    merged[mine, :] = factor

    gathers = []
    for k, b in enumerate(chips):
        send = pltpu.make_async_remote_copy(
            src_ref=merged.at[mine, :],
            dst_ref=merged.at[mine, :],
            send_sem=chip_ssem.at[k],
            recv_sem=chip_rsem.at[k],
            device_id=(b * 2 + core, q),
            device_id_type=MESH,
        )
        send.start()
        gathers.append(send)

    def forward(k, where):
        send = pltpu.make_async_remote_copy(
            src_ref=merged.at[where, :],
            dst_ref=merged.at[where, :],
            send_sem=core_ssem.at[k],
            recv_sem=core_rsem.at[k],
            device_id=partner,
            device_id_type=MESH,
        )
        send.start()
        return send

    relays = [forward(CHIPS - 1, mine)]
    for k in (2, 1, 0):
        gathers[k].wait_recv()
        relays.append(forward(k, quarter(core, chips[k])))
    for send in halves + quarters + gathers:
        send.wait_send()
    for send in relays:
        send.wait()
    final = pltpu.make_async_copy(merged, out_ref, isem.at[0])
    final.start()
    final.wait()


def per_device(estimate, views_data, psf_long, psf_short, detection):
    raw = pl.BlockSpec(memory_space=pl.ANY)
    dma = pltpu.SemaphoreType.DMA
    factor = pl.pallas_call(
        kernel,
        out_shape=jax.ShapeDtypeStruct((L, N), F32),
        in_specs=[raw] * 5,
        out_specs=raw,
        scratch_shapes=[
            pltpu.VMEM((L, N), F32),
            pltpu.VMEM((L, N), F32),
            pltpu.VMEM(psf_long.shape, F32),
            pltpu.VMEM(psf_short.shape, F32),
            pltpu.SMEM(detection.shape, jnp.int32),
            pltpu.VMEM((8, L), F32),
            pltpu.VMEM((2, 2 * L, 4 * L), BF16),
            pltpu.VMEM((2, 4 * L, 2 * L), BF16),
            pltpu.VMEM((2, 2 * L, 4 * L), BF16),
            pltpu.VMEM((2, 2 * L, 4 * L), BF16),
            pltpu.VMEM((N, L), F32),
            pltpu.VMEM((N, L), F32),
            pltpu.VMEM((N, L), F32),
            pltpu.VMEM((N, L), F32),
            pltpu.VMEM((N, L), F32),
            pltpu.VMEM((L, N), F32),
            pltpu.VMEM((CHIPS, YDIM, N), F32),
            pltpu.VMEM((CHIPS - 1, YDIM, N), F32),
            pltpu.VMEM((L, N), F32),
            dma((5,)), dma((2,)), dma((2,)),
            dma((CHIPS,)), dma((CHIPS,)), dma((CHIPS - 1,)), dma((CHIPS - 1,)),
            dma((CHIPS - 1,)), dma((CHIPS - 1,)), dma((CHIPS,)), dma((CHIPS,)),
        ],
        compiler_params=pltpu.CompilerParams(
            collective_id=0, has_side_effects=True
        ),
    )(
        estimate.reshape(L, N),
        views_data.reshape(L, N),
        psf_long,
        psf_short,
        detection,
    )
    return estimate * factor.reshape(estimate.shape)


def solution(mesh):
    return jax.shard_map(
        per_device,
        mesh=mesh,
        in_specs=(
            P("pencil", None, None),
            P("view", "pencil", None, None),
            P("view", None),
            P("view", None, None),
            P("view", None),
        ),
        out_specs=P("pencil", None, None),
        check_vma=False,
    )
```

```python
import functools

import jax
import jax.numpy as jnp
from jax import lax
from jax.experimental import pallas as pl
from jax.experimental.pallas import tpu as pltpu
from jax.sharding import PartitionSpec as P

F32 = jnp.float32
BF16 = jnp.bfloat16
MESH = pl.DeviceIdType.MESH

VIEWS = 8
CHIPS = 4
PENCILS = 64
TILE = 8
N = 512
CHUNKS = 2
HALF = N // CHUNKS
L = 128
YDIM = 16

NN = (((1,), (0,)), ((), ()))
NT = (((1,), (1,)), ((), ()))

OFFSETS = sorted(
    ((a, b, c) for a in range(2) for b in range(8) for c in range(4) if a + b + c),
    key=lambda o: (-(4 * o[0] + min(o[1], 8 - o[1]) + min(o[2], 4 - o[2])), o),
)


def split(a):
    hi = a.astype(BF16)
    lo = (a - hi.astype(F32)).astype(BF16)
    return hi, lo


def dot3(a, b, dims):
    ah, al = a
    bh, bl = b
    dot = functools.partial(
        lax.dot_general, dimension_numbers=dims, preferred_element_type=F32
    )
    return dot(ah, bh) + (dot(ah, bl) + dot(al, bh))


def roll(x, shift, axis):
    return pltpu.roll(x, shift % x.shape[axis], axis)


def shifted(row, amount):
    for bit in range(5):
        flag = ((amount >> bit) & 1) == 1
        row = jnp.where(flag, roll(row, 1 << bit, 1), row)
    return row


def staircase(row, start):
    eight = jnp.broadcast_to(row, (8, row.shape[1]))
    eight = pltpu.roll(eight, 0, 1, stride=1, stride_axis=0)
    return jnp.concatenate([roll(eight, start + 8 * k, 1) for k in range(L // 8)], axis=0)


def band_blocks(row, amount):
    row = shifted(row, amount + 12)
    wide = jnp.concatenate([row, jnp.zeros((1, 2 * L), F32)], axis=1)
    return staircase(wide, 86)


def y_block(row):
    full = staircase(row, 121)
    rows = lax.broadcasted_iota(jnp.int32, (L, L), 0) // YDIM
    cols = lax.broadcasted_iota(jnp.int32, (L, L), 1) // YDIM
    return jnp.where(rows == cols, full, 0.0)


def swap_slab(x):
    x = x.reshape(PENCILS, TILE, L)
    sub = lax.broadcasted_iota(jnp.int32, x.shape, 1)
    lane = lax.broadcasted_iota(jnp.int32, x.shape, 2) // YDIM
    for bit in (4, 2, 1):
        s_bit = (sub // bit) % 2
        same = s_bit == (lane // bit) % 2
        up = roll(roll(x, -bit, 1), YDIM * bit, 2)
        down = up if bit == 4 else roll(roll(x, bit, 1), -YDIM * bit, 2)
        x = jnp.where(same, x, jnp.where(s_bit == 0, up, down))
    return x.reshape(PENCILS * TILE, L)


def taps(long_ref, short_ref, detect_ref, rows):
    rows[...] = jnp.zeros_like(rows)
    rows[0:1, 0 : long_ref.shape[1]] = long_ref[...]
    rows[1:3, 0 : short_ref.shape[2]] = short_ref[0]
    value = rows[...]
    value = value / jnp.maximum(jnp.sum(value, axis=1, keepdims=True), 1e-30)
    along, across, second = value[0:1], roll(value[1:2], 23, 1), value[2:3]
    is_first = detect_ref[0, 0] == 0
    offset = detect_ref[0, 1]
    first = jnp.where(is_first, along, across)
    third = jnp.where(is_first, across, along)
    return (
        (first, jnp.where(is_first, offset, 0)),
        second,
        (third, jnp.where(is_first, 0, offset)),
    )


def store_pair(ref, rows, cols, value):
    hi, lo = split(value)
    ref[0, rows, cols] = hi
    ref[1, rows, cols] = lo


def fill_rows(ref, blocks):
    zero = jnp.zeros((L, L), BF16)
    for part in range(2):
        ref[part, 0:L, 3 * L : 4 * L] = zero
        ref[part, L : 2 * L, 0:L] = zero
    store_pair(ref, slice(0, L), slice(0, 3 * L), blocks)
    store_pair(ref, slice(L, 2 * L), slice(L, 4 * L), blocks)


def fill_cols(ref, blocks):
    zero = jnp.zeros((L, L), BF16)
    left, here, right = (blocks[:, k * L : (k + 1) * L] for k in range(3))
    for part in range(2):
        ref[part, 0:L, L : 2 * L] = zero
        ref[part, 3 * L : 4 * L, 0:L] = zero
    for col in range(2):
        for row, value in enumerate((right, here, left)):
            store_pair(
                ref,
                slice((row + col) * L, (row + col + 1) * L),
                slice(col * L, (col + 1) * L),
                value,
            )


HALVES = ((0, slice(L, 4 * L), slice(0, 3 * L)), (1, slice(0, 3 * L), slice(L, 4 * L)))


def kernel(
    est_hbm, views_hbm, long_hbm, short_hbm, detect_hbm, out_ref,
    est_ref, views_ref, long_ref, short_ref, detect_ref,
    rows, zrow, zcol, xrow, xtrow, views_t,
    send1, recv1, send2, recv2, corr, pair, part, final,
    isem, ssem, rsem, pair_ssem, pair_rsem, part_ssem, part_rsem,
    chip_ssem, chip_rsem, core_ssem, core_rsem,
):
    v = lax.axis_index("view")
    q = lax.axis_index("pencil")
    x, z, yh = q % 4, (q // 4) % 8, q // 32

    def pencil(off):
        a, b, c = off
        return (((yh + a) % 2) * 8 + (z + b) % 8) * 4 + (x + c) % 4

    barrier = pltpu.get_barrier_semaphore()
    for off in OFFSETS:
        pl.semaphore_signal(barrier, inc=1, device_id=(v, pencil(off)), device_id_type=MESH)
    core, chip = v % 2, v // 2
    partner = (chip * 2 + (1 - core), q)
    chips = [(3 - chip) % CHIPS, (chip + 2) % CHIPS, (5 - chip) % CHIPS]
    pl.semaphore_signal(barrier, inc=1, device_id=partner, device_id_type=MESH)
    for other in chips:
        pl.semaphore_signal(
            barrier, inc=1, device_id=(other * 2 + core, q), device_id_type=MESH
        )

    loads = [
        pltpu.make_async_copy(src, dst, isem.at[k])
        for k, (src, dst) in enumerate(
            (
                (long_hbm, long_ref),
                (short_hbm, short_ref),
                (detect_hbm, detect_ref),
                (est_hbm, est_ref),
                (views_hbm, views_ref),
            )
        )
    ]
    for load in loads:
        load.start()
    for load in loads[:3]:
        load.wait()

    (first, first_shift), second, (third, third_shift) = taps(
        long_ref, short_ref, detect_ref, rows
    )
    yb = y_block(second)
    zb = band_blocks(third, third_shift)
    fill_rows(zrow, zb)

    loads[3].wait()
    field = dot3(split(yb), split(est_ref[...]), NN)
    fh, fl = split(field)
    for half, cols, window in HALVES:
        send1[half * 256 : (half + 1) * 256, :] = dot3(
            (zrow[0, :, cols], zrow[1, :, cols]), (fh[:, window], fl[:, window]), NT
        )

    pl.semaphore_wait(barrier, PENCILS - 1 + CHIPS)

    def exchange(src, dst, k):
        mine = pl.ds(pl.multiple_of(q * TILE, TILE), TILE)
        for off in OFFSETS:
            peer = pencil(off)
            pltpu.make_async_remote_copy(
                src_ref=src.at[pl.ds(pl.multiple_of(peer * TILE, TILE), TILE), :],
                dst_ref=dst.at[mine, :],
                send_sem=ssem.at[k],
                recv_sem=rsem.at[k],
                device_id=(v, peer),
                device_id_type=MESH,
            ).start()
        dst[mine, :] = src[mine, :]

    def arrived(src, dst, k, count):
        span = pl.ds(0, count)
        both = pltpu.make_async_copy(src.at[span], dst.at[span], rsem.at[k])
        both.wait()
        pltpu.make_async_copy(src.at[span], dst.at[span], ssem.at[k]).wait()

    exchange(send1, recv1, 0)
    xb = band_blocks(first, first_shift)
    fill_rows(xrow, xb)
    fill_rows(
        xtrow,
        jnp.concatenate([xb[:, k * L : (k + 1) * L].T for k in (2, 1, 0)], axis=1),
    )
    fill_cols(zcol, zb)
    ytb = split(yb.T)
    loads[4].wait()
    views_t[...] = views_ref[...].T
    arrived(send1, recv1, 0, (PENCILS - 1) * TILE)

    gh, gl = split(swap_slab(recv1[...]))
    ratio = []
    for half, cols, window in HALVES:
        blurred = dot3(
            (xrow[0, :, cols], xrow[1, :, cols]), (gh[window], gl[window]), NN
        )
        ratio.append(views_t[half * 256 : (half + 1) * 256, :] / blurred)
    rh, rl = split(jnp.concatenate(ratio, axis=0))
    back = jnp.concatenate(
        [
            dot3((xtrow[0, :, cols], xtrow[1, :, cols]), (rh[window], rl[window]), NN)
            for _, cols, window in HALVES
        ],
        axis=0,
    )
    send2[...] = swap_slab(back)
    exchange(send2, recv2, 1)
    arrived(send2, recv2, 1, (PENCILS - 1) * TILE)

    def quarter(c, b):
        return pl.ds(pl.multiple_of((c * CHIPS + b) * YDIM, YDIM), YDIM)

    def remote(src, dst, sems, index, device):
        send = pltpu.make_async_remote_copy(
            src_ref=src,
            dst_ref=dst,
            send_sem=sems[0].at[index],
            recv_sem=sems[1].at[index],
            device_id=device,
            device_id_type=MESH,
        )
        send.start()
        return send

    order = chips + [chip]
    same_core = [(b * 2 + core, q) for b in chips]
    bh, bl = split(recv2[...].T)
    halves = {}
    for c, (_, rows_, window) in enumerate(HALVES):
        whole = dot3(
            (bh[:, window], bl[:, window]), (zcol[0, rows_, :], zcol[1, rows_, :]), NN
        )
        corr[c] = dot3(ytb, split(whole), NN)
        for k, b in enumerate(order):
            halves[c, k] = remote(
                corr.at[c, quarter(1 - core, b), :], pair.at[c, b],
                (pair_ssem, pair_rsem), c * CHIPS + k, partner,
            )
    quarters = {}
    for c in range(CHUNKS):
        for k, b in enumerate(order):
            halves[c, k].wait_recv()
            pair[c, b] = pair[c, b] * corr[c, quarter(core, b), :]
            if k < CHIPS - 1:
                quarters[c, k] = remote(
                    pair.at[c, b], part.at[c, k],
                    (part_ssem, part_rsem), c * CHIPS + k, same_core[k],
                )
    gathers, locals_, relays = {}, [], []
    mine = quarter(core, chip)
    for c in range(CHUNKS):
        cols = pl.ds(c * HALF, HALF)
        for k in range(CHIPS - 1):
            quarters[c, k].wait_recv()
        final[c] = (pair[c, chip] * part[c, 0]) * (part[c, 1] * part[c, 2])
        target = out_ref.at[mine, cols]
        for k in range(CHIPS - 1):
            gathers[c, k] = remote(
                final.at[c], target, (chip_ssem, chip_rsem), c * CHIPS + k, same_core[k]
            )
        relays.append(
            remote(final.at[c], target, (core_ssem, core_rsem), c * CHIPS + CHIPS - 1, partner)
        )
        local = pltpu.make_async_copy(final.at[c], target, isem.at[c])
        local.start()
        locals_.append(local)
    for c in range(CHUNKS):
        for k in (2, 1, 0):
            gathers[c, k].wait_recv()
            where = out_ref.at[quarter(core, chips[k]), pl.ds(c * HALF, HALF)]
            relays.append(remote(where, where, (core_ssem, core_rsem), c * CHIPS + k, partner))
    for sends in (halves, quarters, gathers):
        for send in sends.values():
            send.wait_send()
    for send in relays + locals_:
        send.wait()


def per_device(estimate, views_data, psf_long, psf_short, detection):
    raw = pl.BlockSpec(memory_space=pl.ANY)
    dma = pltpu.SemaphoreType.DMA
    factor = pl.pallas_call(
        kernel,
        out_shape=jax.ShapeDtypeStruct((L, N), F32),
        in_specs=[raw] * 5,
        out_specs=raw,
        scratch_shapes=[
            pltpu.VMEM((L, N), F32),
            pltpu.VMEM((L, N), F32),
            pltpu.VMEM(psf_long.shape, F32),
            pltpu.VMEM(psf_short.shape, F32),
            pltpu.SMEM(detection.shape, jnp.int32),
            pltpu.VMEM((8, L), F32),
            pltpu.VMEM((2, 2 * L, 4 * L), BF16),
            pltpu.VMEM((2, 4 * L, 2 * L), BF16),
            pltpu.VMEM((2, 2 * L, 4 * L), BF16),
            pltpu.VMEM((2, 2 * L, 4 * L), BF16),
            pltpu.VMEM((N, L), F32),
            pltpu.VMEM((N, L), F32),
            pltpu.VMEM((N, L), F32),
            pltpu.VMEM((N, L), F32),
            pltpu.VMEM((N, L), F32),
            pltpu.VMEM((CHUNKS, L, HALF), F32),
            pltpu.VMEM((CHUNKS, CHIPS, YDIM, HALF), F32),
            pltpu.VMEM((CHUNKS, CHIPS - 1, YDIM, HALF), F32),
            pltpu.VMEM((CHUNKS, YDIM, HALF), F32),
            dma((5,)), dma((2,)), dma((2,)),
            *[dma((CHUNKS * CHIPS,))] * 8,
        ],
        compiler_params=pltpu.CompilerParams(
            collective_id=0, has_side_effects=True, vmem_limit_bytes=32 << 20
        ),
    )(
        *(
            pltpu.with_memory_space_constraint(a, pltpu.HBM)
            for a in (
                estimate.reshape(L, N),
                views_data.reshape(L, N),
                psf_long,
                psf_short,
                detection,
            )
        )
    )
    return estimate * factor.reshape(estimate.shape)


def solution(mesh):
    return jax.shard_map(
        per_device,
        mesh=mesh,
        in_specs=(
            P("pencil", None, None),
            P("view", "pencil", None, None),
            P("view", None),
            P("view", None, None),
            P("view", None),
        ),
        out_specs=P("pencil", None, None),
        check_vma=False,
    )
```

```python
import functools

import jax
import jax.numpy as jnp
from jax import lax
from jax.experimental import pallas as pl
from jax.experimental.pallas import tpu as pltpu
from jax.sharding import PartitionSpec as P

F32 = jnp.float32
BF16 = jnp.bfloat16
MESH = pl.DeviceIdType.MESH

VIEWS = 8
CHIPS = 4
PENCILS = 64
TILE = 8
N = 512
CHUNKS = 2
HALF = N // CHUNKS
L = 128
YDIM = 16

NN = (((1,), (0,)), ((), ()))
NT = (((1,), (1,)), ((), ()))

OFFSETS = sorted(
    ((a, b, c) for a in range(2) for b in range(8) for c in range(4) if a + b + c),
    key=lambda o: (-(4 * o[0] + min(o[1], 8 - o[1]) + min(o[2], 4 - o[2])), o),
)


def split(a):
    hi = a.astype(BF16)
    lo = (a - hi.astype(F32)).astype(BF16)
    return hi, lo


def dot3(a, b, dims):
    ah, al = a
    bh, bl = b
    dot = functools.partial(
        lax.dot_general, dimension_numbers=dims, preferred_element_type=F32
    )
    return dot(ah, bh) + (dot(ah, bl) + dot(al, bh))


def roll(x, shift, axis):
    return pltpu.roll(x, shift % x.shape[axis], axis)


def shifted(row, amount):
    for bit in range(5):
        flag = ((amount >> bit) & 1) == 1
        row = jnp.where(flag, roll(row, 1 << bit, 1), row)
    return row


def staircase(row, start):
    eight = jnp.broadcast_to(row, (8, row.shape[1]))
    eight = pltpu.roll(eight, 0, 1, stride=1, stride_axis=0)
    return jnp.concatenate([roll(eight, start + 8 * k, 1) for k in range(L // 8)], axis=0)


def band_blocks(row, amount):
    row = shifted(row, amount + 12)
    wide = jnp.concatenate([row, jnp.zeros((1, 2 * L), F32)], axis=1)
    return staircase(wide, 86)


def y_block(row):
    full = staircase(row, 121)
    rows = lax.broadcasted_iota(jnp.int32, (L, L), 0) // YDIM
    cols = lax.broadcasted_iota(jnp.int32, (L, L), 1) // YDIM
    return jnp.where(rows == cols, full, 0.0)


def swap_slab(x):
    rows = x.shape[0]
    x = x.reshape(rows // TILE, TILE, L)
    sub = lax.broadcasted_iota(jnp.int32, x.shape, 1)
    lane = lax.broadcasted_iota(jnp.int32, x.shape, 2) // YDIM
    for bit in (4, 2, 1):
        s_bit = (sub // bit) % 2
        same = s_bit == (lane // bit) % 2
        up = roll(roll(x, -bit, 1), YDIM * bit, 2)
        down = up if bit == 4 else roll(roll(x, bit, 1), -YDIM * bit, 2)
        x = jnp.where(same, x, jnp.where(s_bit == 0, up, down))
    return x.reshape(rows, L)


def taps(long_ref, short_ref, detect_ref, rows):
    rows[...] = jnp.zeros_like(rows)
    rows[0:1, 0 : long_ref.shape[1]] = long_ref[...]
    rows[1:3, 0 : short_ref.shape[2]] = short_ref[0]
    value = rows[...]
    value = value / jnp.maximum(jnp.sum(value, axis=1, keepdims=True), 1e-30)
    along, across, second = value[0:1], roll(value[1:2], 23, 1), value[2:3]
    is_first = detect_ref[0, 0] == 0
    offset = detect_ref[0, 1]
    first = jnp.where(is_first, along, across)
    third = jnp.where(is_first, across, along)
    return (
        (first, jnp.where(is_first, offset, 0)),
        second,
        (third, jnp.where(is_first, 0, offset)),
    )


def store_pair(ref, rows, cols, value):
    hi, lo = split(value)
    ref[0, rows, cols] = hi
    ref[1, rows, cols] = lo


def fill_rows(ref, blocks):
    zero = jnp.zeros((L, L), BF16)
    for part in range(2):
        ref[part, 0:L, 3 * L : 4 * L] = zero
        ref[part, L : 2 * L, 0:L] = zero
    store_pair(ref, slice(0, L), slice(0, 3 * L), blocks)
    store_pair(ref, slice(L, 2 * L), slice(L, 4 * L), blocks)


def fill_cols(ref, blocks):
    zero = jnp.zeros((L, L), BF16)
    left, here, right = (blocks[:, k * L : (k + 1) * L] for k in range(3))
    for part in range(2):
        ref[part, 0:L, L : 2 * L] = zero
        ref[part, 3 * L : 4 * L, 0:L] = zero
    for col in range(2):
        for row, value in enumerate((right, here, left)):
            store_pair(
                ref,
                slice((row + col) * L, (row + col + 1) * L),
                slice(col * L, (col + 1) * L),
                value,
            )


def fill_halves(ref, blocks):
    zero = jnp.zeros((L, L), BF16)
    for part in range(2):
        ref[part, 0, 0:L, 2 * L : 3 * L] = zero
        ref[part, 1, L : 2 * L, 0:L] = zero
    for part, value in enumerate(split(blocks)):
        ref[part, 0, 0:L, 0 : 2 * L] = value[:, L : 3 * L]
        ref[part, 0, L : 2 * L, :] = value
        ref[part, 1, 0:L, :] = value
        ref[part, 1, L : 2 * L, L : 3 * L] = value[:, 0 : 2 * L]


HALVES = ((0, slice(L, 4 * L), slice(0, 3 * L)), (1, slice(0, 3 * L), slice(L, 4 * L)))


def kernel(
    est_hbm, views_hbm, long_hbm, short_hbm, detect_hbm, out_ref,
    est_ref, views_ref, long_ref, short_ref, detect_ref,
    rows, zrow, zcol, xrow, xtrow, views_t,
    send1, recv1, send2, recv2, lines, ratio, turned, corr, pair, part, final,
    isem, ssem, rsem, pair_ssem, pair_rsem, part_ssem, part_rsem,
    chip_ssem, chip_rsem, core_ssem, core_rsem,
):
    v = lax.axis_index("view")
    q = lax.axis_index("pencil")
    x, z, yh = q % 4, (q // 4) % 8, q // 32

    def pencil(off):
        a, b, c = off
        return (((yh + a) % 2) * 8 + (z + b) % 8) * 4 + (x + c) % 4

    barrier = pltpu.get_barrier_semaphore()
    for off in OFFSETS:
        pl.semaphore_signal(barrier, inc=1, device_id=(v, pencil(off)), device_id_type=MESH)
    core, chip = v % 2, v // 2
    partner = (chip * 2 + (1 - core), q)
    chips = [(3 - chip) % CHIPS, (chip + 2) % CHIPS, (5 - chip) % CHIPS]
    pl.semaphore_signal(barrier, inc=1, device_id=partner, device_id_type=MESH)
    for other in chips:
        pl.semaphore_signal(
            barrier, inc=1, device_id=(other * 2 + core, q), device_id_type=MESH
        )

    loads = [
        pltpu.make_async_copy(src, dst, isem.at[k])
        for k, (src, dst) in enumerate(
            (
                (long_hbm, long_ref),
                (short_hbm, short_ref),
                (detect_hbm, detect_ref),
                (est_hbm, est_ref),
                (views_hbm, views_ref),
            )
        )
    ]
    for load in loads:
        load.start()
    for load in loads[:3]:
        load.wait()

    (first, first_shift), second, (third, third_shift) = taps(
        long_ref, short_ref, detect_ref, rows
    )
    yb = y_block(second)
    zb = band_blocks(third, third_shift)
    fill_rows(zrow, zb)

    loads[3].wait()
    field = dot3(split(yb), split(est_ref[...]), NN)
    fh, fl = split(field)
    for half, cols, window in HALVES:
        send1[half * 256 : (half + 1) * 256, :] = dot3(
            (zrow[0, :, cols], zrow[1, :, cols]), (fh[:, window], fl[:, window]), NT
        )

    pl.semaphore_wait(barrier, PENCILS - 1 + CHIPS)

    def exchange(src, dst, k, far):
        mine = pl.ds(pl.multiple_of(q * TILE, TILE), TILE)
        for off in OFFSETS:
            if off[0] != far:
                continue
            peer = pencil(off)
            pltpu.make_async_remote_copy(
                src_ref=src.at[pl.ds(pl.multiple_of(peer * TILE, TILE), TILE), :],
                dst_ref=dst.at[mine, :],
                send_sem=ssem.at[2 * k + far],
                recv_sem=rsem.at[2 * k + far],
                device_id=(v, peer),
                device_id_type=MESH,
            ).start()
        if not far:
            dst[mine, :] = src[mine, :]

    def count(far):
        return pl.ds(0, (PENCILS // 2 - 1 + far) * TILE)

    def arrived(dst, k, far):
        view = dst.at[count(far), :]
        pltpu.make_async_copy(view, view, rsem.at[2 * k + far]).wait()

    def sent(src, k):
        for far in range(2):
            view = src.at[count(far), :]
            pltpu.make_async_copy(view, view, ssem.at[2 * k + far]).wait()

    def half_rows(half):
        return pl.ds(pl.multiple_of(half * 2 * L, 2 * L), 2 * L)

    planes = (yh, (yh + 1) % 2)

    for far in (1, 0):
        exchange(send1, recv1, 0, far)
    xb = band_blocks(first, first_shift)
    fill_rows(xrow, xb)
    fill_halves(
        xtrow,
        jnp.concatenate([xb[:, k * L : (k + 1) * L].T for k in (2, 1, 0)], axis=1),
    )
    fill_cols(zcol, zb)
    ytb = split(yb.T)
    loads[4].wait()
    views_t[...] = views_ref[...].T

    for far in range(2):
        arrived(recv1, 0, far)
        rows_ = half_rows(planes[far])
        for k, value in enumerate(split(swap_slab(recv1[rows_, :]))):
            lines[k, rows_, :] = value
    for half, cols, window in HALVES:
        blurred = dot3(
            (xrow[0, :, cols], xrow[1, :, cols]),
            (lines[0, window, :], lines[1, window, :]),
            NN,
        )
        rows_ = slice(half * 2 * L, (half + 1) * 2 * L)
        for k, value in enumerate(split(views_t[rows_, :] / blurred)):
            ratio[k, rows_, :] = value
    for far in (1, 0):
        half = planes[far]
        window = pl.ds(pl.multiple_of(half * L, L), 3 * L)
        back = dot3(
            (xtrow[0, half], xtrow[1, half]), (ratio[0, window, :], ratio[1, window, :]), NN
        )
        send2[half_rows(half), :] = swap_slab(back)
        exchange(send2, recv2, 1, far)
    for far in range(2):
        arrived(recv2, 1, far)
        part_ = dot3(ytb, split(recv2[half_rows(planes[far]), :]), NT)
        for k, value in enumerate(split(part_)):
            turned[k, planes[far]] = value

    def quarter(c, b):
        return pl.ds(pl.multiple_of((c * CHIPS + b) * YDIM, YDIM), YDIM)

    def remote(src, dst, sems, index, device):
        send = pltpu.make_async_remote_copy(
            src_ref=src,
            dst_ref=dst,
            send_sem=sems[0].at[index],
            recv_sem=sems[1].at[index],
            device_id=device,
            device_id_type=MESH,
        )
        send.start()
        return send

    order = chips + [chip]
    same_core = [(b * 2 + core, q) for b in chips]
    bh, bl = (jnp.concatenate([turned[k, 0], turned[k, 1]], axis=1) for k in range(2))
    halves = {}
    for c, (_, rows_, window) in enumerate(HALVES):
        corr[c] = dot3(
            (bh[:, window], bl[:, window]), (zcol[0, rows_, :], zcol[1, rows_, :]), NN
        )
        for k, b in enumerate(order):
            halves[c, k] = remote(
                corr.at[c, quarter(1 - core, b), :], pair.at[c, b],
                (pair_ssem, pair_rsem), c * CHIPS + k, partner,
            )
    quarters = {}
    for c in range(CHUNKS):
        for k, b in enumerate(order):
            halves[c, k].wait_recv()
            pair[c, b] = pair[c, b] * corr[c, quarter(core, b), :]
            if k < CHIPS - 1:
                quarters[c, k] = remote(
                    pair.at[c, b], part.at[c, k],
                    (part_ssem, part_rsem), c * CHIPS + k, same_core[k],
                )
    gathers, locals_, relays = {}, [], []
    mine = quarter(core, chip)
    for c in range(CHUNKS):
        cols = pl.ds(c * HALF, HALF)
        for k in range(CHIPS - 1):
            quarters[c, k].wait_recv()
        final[c] = (pair[c, chip] * part[c, 0]) * (part[c, 1] * part[c, 2])
        target = out_ref.at[mine, cols]
        for k in range(CHIPS - 1):
            gathers[c, k] = remote(
                final.at[c], target, (chip_ssem, chip_rsem), c * CHIPS + k, same_core[k]
            )
        relays.append(
            remote(final.at[c], target, (core_ssem, core_rsem), c * CHIPS + CHIPS - 1, partner)
        )
        local = pltpu.make_async_copy(final.at[c], target, isem.at[c])
        local.start()
        locals_.append(local)
    for c in range(CHUNKS):
        for k in (2, 1, 0):
            gathers[c, k].wait_recv()
            where = out_ref.at[quarter(core, chips[k]), pl.ds(c * HALF, HALF)]
            relays.append(remote(where, where, (core_ssem, core_rsem), c * CHIPS + k, partner))
    sent(send1, 0)
    sent(send2, 1)
    for sends in (halves, quarters, gathers):
        for send in sends.values():
            send.wait_send()
    for send in relays + locals_:
        send.wait()


def per_device(estimate, views_data, psf_long, psf_short, detection):
    raw = pl.BlockSpec(memory_space=pl.ANY)
    dma = pltpu.SemaphoreType.DMA
    factor = pl.pallas_call(
        kernel,
        out_shape=jax.ShapeDtypeStruct((L, N), F32),
        in_specs=[raw] * 5,
        out_specs=raw,
        scratch_shapes=[
            pltpu.VMEM((L, N), F32),
            pltpu.VMEM((L, N), F32),
            pltpu.VMEM(psf_long.shape, F32),
            pltpu.VMEM(psf_short.shape, F32),
            pltpu.SMEM(detection.shape, jnp.int32),
            pltpu.VMEM((8, L), F32),
            pltpu.VMEM((2, 2 * L, 4 * L), BF16),
            pltpu.VMEM((2, 4 * L, 2 * L), BF16),
            pltpu.VMEM((2, 2 * L, 4 * L), BF16),
            pltpu.VMEM((2, 2, 2 * L, 3 * L), BF16),
            pltpu.VMEM((N, L), F32),
            pltpu.VMEM((N, L), F32),
            pltpu.VMEM((N, L), F32),
            pltpu.VMEM((N, L), F32),
            pltpu.VMEM((N, L), F32),
            pltpu.VMEM((2, N, L), BF16),
            pltpu.VMEM((2, N, L), BF16),
            pltpu.VMEM((2, 2, L, 2 * L), BF16),
            pltpu.VMEM((CHUNKS, L, HALF), F32),
            pltpu.VMEM((CHUNKS, CHIPS, YDIM, HALF), F32),
            pltpu.VMEM((CHUNKS, CHIPS - 1, YDIM, HALF), F32),
            pltpu.VMEM((CHUNKS, YDIM, HALF), F32),
            dma((5,)), dma((4,)), dma((4,)),
            *[dma((CHUNKS * CHIPS,))] * 8,
        ],
        compiler_params=pltpu.CompilerParams(
            collective_id=0, has_side_effects=True, vmem_limit_bytes=32 << 20
        ),
    )(
        *(
            pltpu.with_memory_space_constraint(a, pltpu.HBM)
            for a in (
                estimate.reshape(L, N),
                views_data.reshape(L, N),
                psf_long,
                psf_short,
                detection,
            )
        )
    )
    return estimate * factor.reshape(estimate.shape)


def solution(mesh):
    return jax.shard_map(
        per_device,
        mesh=mesh,
        in_specs=(
            P("pencil", None, None),
            P("view", "pencil", None, None),
            P("view", None),
            P("view", None, None),
            P("view", None),
        ),
        out_specs=P("pencil", None, None),
        check_vma=False,
    )
```

```python
import functools

import jax
import jax.numpy as jnp
from jax import lax
from jax.experimental import pallas as pl
from jax.experimental.pallas import tpu as pltpu
from jax.sharding import PartitionSpec as P

F32 = jnp.float32
BF16 = jnp.bfloat16
MESH = pl.DeviceIdType.MESH

VIEWS = 8
CHIPS = 4
PENCILS = 64
TILE = 8
N = 512
CHUNKS = 2
HALF = N // CHUNKS
L = 128
YDIM = 16
ROWS = L // 4

NN = (((1,), (0,)), ((), ()))
NT = (((1,), (1,)), ((), ()))

OFFSETS = sorted(
    ((a, b, c) for a in range(2) for b in range(8) for c in range(4) if a + b + c),
    key=lambda o: (-(4 * o[0] + min(o[1], 8 - o[1]) + min(o[2], 4 - o[2])), o),
)


def split(a):
    hi = a.astype(BF16)
    lo = (a - hi.astype(F32)).astype(BF16)
    return hi, lo


def dot3(a, b, dims):
    ah, al = a
    bh, bl = b
    dot = functools.partial(
        lax.dot_general, dimension_numbers=dims, preferred_element_type=F32
    )
    return dot(ah, bh) + (dot(ah, bl) + dot(al, bh))


def roll(x, shift, axis):
    return pltpu.roll(x, shift % x.shape[axis], axis)


def shifted(row, amount):
    for bit in range(5):
        flag = ((amount >> bit) & 1) == 1
        row = jnp.where(flag, roll(row, 1 << bit, 1), row)
    return row


def staircase(row, start):
    eight = jnp.broadcast_to(row, (8, row.shape[1]))
    eight = pltpu.roll(eight, 0, 1, stride=1, stride_axis=0)
    return jnp.concatenate([roll(eight, start + 8 * k, 1) for k in range(L // 8)], axis=0)


def band_blocks(row, amount):
    row = shifted(row, amount + 12)
    wide = jnp.concatenate([row, jnp.zeros((1, 2 * L), F32)], axis=1)
    return staircase(wide, 86)


def y_block(row):
    full = staircase(row, 121)
    rows = lax.broadcasted_iota(jnp.int32, (L, L), 0) // YDIM
    cols = lax.broadcasted_iota(jnp.int32, (L, L), 1) // YDIM
    return jnp.where(rows == cols, full, 0.0)


def swap_slab(x):
    rows = x.shape[0]
    x = x.reshape(rows // TILE, TILE, L)
    sub = lax.broadcasted_iota(jnp.int32, x.shape, 1)
    lane = lax.broadcasted_iota(jnp.int32, x.shape, 2) // YDIM
    for bit in (4, 2, 1):
        s_bit = (sub // bit) % 2
        same = s_bit == (lane // bit) % 2
        up = roll(roll(x, -bit, 1), YDIM * bit, 2)
        down = up if bit == 4 else roll(roll(x, bit, 1), -YDIM * bit, 2)
        x = jnp.where(same, x, jnp.where(s_bit == 0, up, down))
    return x.reshape(rows, L)


def taps(long_ref, short_ref, detect_ref, rows):
    rows[...] = jnp.zeros_like(rows)
    rows[0:1, 0 : long_ref.shape[1]] = long_ref[...]
    rows[1:3, 0 : short_ref.shape[2]] = short_ref[0]
    value = rows[...]
    value = value / jnp.maximum(jnp.sum(value, axis=1, keepdims=True), 1e-30)
    along, across, second = value[0:1], roll(value[1:2], 23, 1), value[2:3]
    is_first = detect_ref[0, 0] == 0
    offset = detect_ref[0, 1]
    first = jnp.where(is_first, along, across)
    third = jnp.where(is_first, across, along)
    return (
        (first, jnp.where(is_first, offset, 0)),
        second,
        (third, jnp.where(is_first, 0, offset)),
    )


def store_pair(ref, rows, cols, value):
    hi, lo = split(value)
    ref[0, rows, cols] = hi
    ref[1, rows, cols] = lo


def fill_rows(ref, blocks):
    zero = jnp.zeros((L, L), BF16)
    for part in range(2):
        ref[part, 0:L, 3 * L : 4 * L] = zero
        ref[part, L : 2 * L, 0:L] = zero
    store_pair(ref, slice(0, L), slice(0, 3 * L), blocks)
    store_pair(ref, slice(L, 2 * L), slice(L, 4 * L), blocks)


def fill_cols(ref, blocks):
    zero = jnp.zeros((L, L), BF16)
    left, here, right = (blocks[:, k * L : (k + 1) * L] for k in range(3))
    for part in range(2):
        ref[part, 0:L, L : 2 * L] = zero
        ref[part, 3 * L : 4 * L, 0:L] = zero
    for col in range(2):
        for row, value in enumerate((right, here, left)):
            store_pair(
                ref,
                slice((row + col) * L, (row + col + 1) * L),
                slice(col * L, (col + 1) * L),
                value,
            )


def fill_halves(ref, blocks):
    zero = jnp.zeros((L, L), BF16)
    for part in range(2):
        ref[part, 0, 0:L, 2 * L : 3 * L] = zero
        ref[part, 1, L : 2 * L, 0:L] = zero
    for part, value in enumerate(split(blocks)):
        ref[part, 0, 0:L, 0 : 2 * L] = value[:, L : 3 * L]
        ref[part, 0, L : 2 * L, :] = value
        ref[part, 1, 0:L, :] = value
        ref[part, 1, L : 2 * L, L : 3 * L] = value[:, 0 : 2 * L]


HALVES = ((0, slice(L, 4 * L), slice(0, 3 * L)), (1, slice(0, 3 * L), slice(L, 4 * L)))


def kernel(
    est_hbm, views_hbm, long_hbm, short_hbm, detect_hbm, out_ref,
    est_ref, views_ref, long_ref, short_ref, detect_ref,
    rows, zrow, zcol, xrow, xtrow, views_t,
    send1, recv1, send2, recv2, lines, ratio, turned, corr, pair, part, final,
    isem, ssem, rsem, pair_ssem, pair_rsem, part_ssem, part_rsem,
    chip_ssem, chip_rsem, core_ssem, core_rsem,
):
    v = lax.axis_index("view")
    q = lax.axis_index("pencil")
    x, z, yh = q % 4, (q // 4) % 8, q // 32

    def pencil(off):
        a, b, c = off
        return (((yh + a) % 2) * 8 + (z + b) % 8) * 4 + (x + c) % 4

    barrier = pltpu.get_barrier_semaphore()
    for off in OFFSETS:
        pl.semaphore_signal(barrier, inc=1, device_id=(v, pencil(off)), device_id_type=MESH)
    core, chip = v % 2, v // 2
    partner = (chip * 2 + (1 - core), q)
    chips = [(3 - chip) % CHIPS, (chip + 2) % CHIPS, (5 - chip) % CHIPS]
    pl.semaphore_signal(barrier, inc=1, device_id=partner, device_id_type=MESH)
    for other in chips:
        pl.semaphore_signal(
            barrier, inc=1, device_id=(other * 2 + core, q), device_id_type=MESH
        )

    loads = [
        pltpu.make_async_copy(src, dst, isem.at[k])
        for k, (src, dst) in enumerate(
            (
                (long_hbm, long_ref),
                (short_hbm, short_ref),
                (detect_hbm, detect_ref),
                (est_hbm, est_ref),
                (views_hbm, views_ref),
            )
        )
    ]
    for load in loads:
        load.start()
    for load in loads[:3]:
        load.wait()

    (first, first_shift), second, (third, third_shift) = taps(
        long_ref, short_ref, detect_ref, rows
    )
    yb = y_block(second)
    zb = band_blocks(third, third_shift)
    fill_rows(zrow, zb)

    loads[3].wait()
    field = dot3(split(yb), split(est_ref[...]), NN)
    fh, fl = split(field)
    for half, cols, window in HALVES:
        send1[half * 256 : (half + 1) * 256, :] = dot3(
            (zrow[0, :, cols], zrow[1, :, cols]), (fh[:, window], fl[:, window]), NT
        )

    pl.semaphore_wait(barrier, PENCILS - 1 + CHIPS)

    def exchange(src, dst, k, far):
        mine = pl.ds(pl.multiple_of(q * TILE, TILE), TILE)
        for off in OFFSETS:
            if off[0] != far:
                continue
            peer = pencil(off)
            pltpu.make_async_remote_copy(
                src_ref=src.at[pl.ds(pl.multiple_of(peer * TILE, TILE), TILE), :],
                dst_ref=dst.at[mine, :],
                send_sem=ssem.at[2 * k + far],
                recv_sem=rsem.at[2 * k + far],
                device_id=(v, peer),
                device_id_type=MESH,
            ).start()
        if not far:
            dst[mine, :] = src[mine, :]

    def count(far):
        return pl.ds(0, (PENCILS // 2 - 1 + far) * TILE)

    def arrived(dst, k, far):
        view = dst.at[count(far), :]
        pltpu.make_async_copy(view, view, rsem.at[2 * k + far]).wait()

    def sent(src, k):
        for far in range(2):
            view = src.at[count(far), :]
            pltpu.make_async_copy(view, view, ssem.at[2 * k + far]).wait()

    def half_rows(half):
        return pl.ds(pl.multiple_of(half * 2 * L, 2 * L), 2 * L)

    planes = (yh, (yh + 1) % 2)

    for far in (1, 0):
        exchange(send1, recv1, 0, far)
    xb = band_blocks(first, first_shift)
    fill_rows(xrow, xb)
    fill_halves(
        xtrow,
        jnp.concatenate([xb[:, k * L : (k + 1) * L].T for k in (2, 1, 0)], axis=1),
    )
    fill_cols(zcol, zb)
    ytb = split(yb.T)
    loads[4].wait()
    views_t[...] = views_ref[...].T

    for far in range(2):
        arrived(recv1, 0, far)
        rows_ = half_rows(planes[far])
        for k, value in enumerate(split(swap_slab(recv1[rows_, :]))):
            lines[k, rows_, :] = value
    for half, cols, window in HALVES:
        blurred = dot3(
            (xrow[0, :, cols], xrow[1, :, cols]),
            (lines[0, window, :], lines[1, window, :]),
            NN,
        )
        rows_ = slice(half * 2 * L, (half + 1) * 2 * L)
        for k, value in enumerate(split(views_t[rows_, :] / blurred)):
            ratio[k, rows_, :] = value
    for far in (1, 0):
        half = planes[far]
        window = pl.ds(pl.multiple_of(half * L, L), 3 * L)
        back = dot3(
            (xtrow[0, half], xtrow[1, half]), (ratio[0, window, :], ratio[1, window, :]), NN
        )
        send2[half_rows(half), :] = swap_slab(back)
        exchange(send2, recv2, 1, far)
    for far in range(2):
        arrived(recv2, 1, far)
        part_ = dot3(ytb, split(recv2[half_rows(planes[far]), :]), NT)
        for k, value in enumerate(split(part_)):
            turned[k, planes[far]] = value

    outer = 1 - ((chip + 1) // 2) % 2
    away, home = 1 - chip // 2, chip // 2

    def owned(c, o):
        return pl.ds(pl.multiple_of((c * 2 + o) * ROWS, ROWS), ROWS)

    def on_chip(b):
        return (b * 2 + core, q)

    def remote(src, dst, sends, send, recvs, recv, device):
        return pltpu.make_async_remote_copy(
            src_ref=src,
            dst_ref=dst,
            send_sem=sends.at[send],
            recv_sem=recvs.at[recv],
            device_id=device,
            device_id_type=MESH,
        )

    def swap(c, k, o):
        return remote(
            corr.at[c, owned(1 - core, o), :], pair.at[c, o],
            pair_ssem, 2 * c + k, pair_rsem, 2 * c + k, partner,
        )

    def collect(c, k, o, slot):
        return remote(
            pair.at[c, o], part.at[c, slot],
            part_ssem, 2 * c + k, part_rsem, 3 * c + slot, on_chip(1 + o),
        )

    def place(c, o):
        return out_ref.at[owned(core, o), pl.ds(c * HALF, HALF)]

    def spread(c, k):
        target = ((3 * (2 - chip)) % CHIPS, 3 - chip, (3 * (chip - 1)) % CHIPS)[k]
        return remote(
            final.at[c], place(c, home),
            chip_ssem, 3 * c + k, chip_rsem, 2 * c + home, on_chip(target),
        )

    def landed(c, o):
        return remote(
            final.at[c], place(c, o), chip_ssem, 3 * c, chip_rsem, 2 * c + o, partner
        )

    def share(c, o):
        return remote(
            place(c, o), place(c, o), core_ssem, 2 * c + o, core_rsem, 2 * c + o, partner
        )

    def share_own(c):
        return remote(
            final.at[c], place(c, home),
            core_ssem, 2 * c + home, core_rsem, 2 * c + home, partner,
        )

    def keep(c):
        return pltpu.make_async_copy(final.at[c], place(c, home), isem.at[c])

    bh, bl = (jnp.concatenate([turned[k, 0], turned[k, 1]], axis=1) for k in range(2))
    for c, (_, rows_, window) in enumerate(HALVES):
        corr[c] = dot3(
            (bh[:, window], bl[:, window]), (zcol[0, rows_, :], zcol[1, rows_, :]), NN
        )
        for k, o in enumerate((away, home)):
            swap(c, k, o).start()
    for c in range(CHUNKS):
        for k, o in enumerate((away, home)):
            swap(c, k, o).wait_recv()
            pair[c, o] = pair[c, o] * corr[c, owned(core, o), :]
            if k == 0:
                collect(c, k, o, 1 - outer).start()
            else:

                @pl.when(outer == 1)
                def _():
                    collect(c, k, o, 2).start()

    @pl.when(outer == 0)
    def _():
        for c in range(CHUNKS):
            for slot in range(3):
                collect(c, 0, home, slot).wait_recv()
            final[c] = (pair[c, home] * part[c, 0]) * (part[c, 1] * part[c, 2])
            for k in range(3):
                spread(c, k).start()
            share_own(c).start()
            keep(c).start()

    for c in range(CHUNKS):
        landed(c, away).wait_recv()
        share(c, away).start()

        @pl.when(outer == 1)
        def _():
            landed(c, home).wait_recv()
            share(c, home).start()

    sent(send1, 0)
    sent(send2, 1)
    for c in range(CHUNKS):
        for k, o in enumerate((away, home)):
            swap(c, k, o).wait_send()
        collect(c, 0, away, 0).wait_send()

        @pl.when(outer == 1)
        def _():
            collect(c, 1, home, 2).wait_send()

        @pl.when(outer == 0)
        def _():
            for k in range(3):
                spread(c, k).wait_send()
            keep(c).wait()

        for o in (away, home):
            share(c, o).wait()


def per_device(estimate, views_data, psf_long, psf_short, detection):
    raw = pl.BlockSpec(memory_space=pl.ANY)
    dma = pltpu.SemaphoreType.DMA
    factor = pl.pallas_call(
        kernel,
        out_shape=jax.ShapeDtypeStruct((L, N), F32),
        in_specs=[raw] * 5,
        out_specs=raw,
        scratch_shapes=[
            pltpu.VMEM((L, N), F32),
            pltpu.VMEM((L, N), F32),
            pltpu.VMEM(psf_long.shape, F32),
            pltpu.VMEM(psf_short.shape, F32),
            pltpu.SMEM(detection.shape, jnp.int32),
            pltpu.VMEM((8, L), F32),
            pltpu.VMEM((2, 2 * L, 4 * L), BF16),
            pltpu.VMEM((2, 4 * L, 2 * L), BF16),
            pltpu.VMEM((2, 2 * L, 4 * L), BF16),
            pltpu.VMEM((2, 2, 2 * L, 3 * L), BF16),
            pltpu.VMEM((N, L), F32),
            pltpu.VMEM((N, L), F32),
            pltpu.VMEM((N, L), F32),
            pltpu.VMEM((N, L), F32),
            pltpu.VMEM((N, L), F32),
            pltpu.VMEM((2, N, L), BF16),
            pltpu.VMEM((2, N, L), BF16),
            pltpu.VMEM((2, 2, L, 2 * L), BF16),
            pltpu.VMEM((CHUNKS, L, HALF), F32),
            pltpu.VMEM((CHUNKS, 2, ROWS, HALF), F32),
            pltpu.VMEM((CHUNKS, CHIPS - 1, ROWS, HALF), F32),
            pltpu.VMEM((CHUNKS, ROWS, HALF), F32),
            dma((5,)), dma((4,)), dma((4,)),
            dma((CHUNKS * 2,)), dma((CHUNKS * 2,)), dma((CHUNKS * 2,)), dma((CHUNKS * 3,)),
            dma((CHUNKS * 3,)), dma((CHUNKS * 2,)), dma((CHUNKS * 2,)), dma((CHUNKS * 2,)),
        ],
        compiler_params=pltpu.CompilerParams(
            collective_id=0, has_side_effects=True, vmem_limit_bytes=32 << 20
        ),
    )(
        *(
            pltpu.with_memory_space_constraint(a, pltpu.HBM)
            for a in (
                estimate.reshape(L, N),
                views_data.reshape(L, N),
                psf_long,
                psf_short,
                detection,
            )
        )
    )
    return estimate * factor.reshape(estimate.shape)


def solution(mesh):
    return jax.shard_map(
        per_device,
        mesh=mesh,
        in_specs=(
            P("pencil", None, None),
            P("view", "pencil", None, None),
            P("view", None),
            P("view", None, None),
            P("view", None),
        ),
        out_specs=P("pencil", None, None),
        check_vma=False,
    )
```

```python
import functools

import jax
import jax.numpy as jnp
from jax import lax
from jax.experimental import pallas as pl
from jax.experimental.pallas import tpu as pltpu
from jax.sharding import PartitionSpec as P

F32 = jnp.float32
BF16 = jnp.bfloat16
MESH = pl.DeviceIdType.MESH

VIEWS = 8
CHIPS = 4
PENCILS = 64
TILE = 8
N = 512
CHUNKS = 2
HALF = N // CHUNKS
L = 128
EDGE = 64
YDIM = 16

NN = (((1,), (0,)), ((), ()))
NT = (((1,), (1,)), ((), ()))

OFFSETS = sorted(
    ((a, b, c) for a in range(2) for b in range(8) for c in range(4) if a + b + c),
    key=lambda o: (-(4 * o[0] + min(o[1], 8 - o[1]) + min(o[2], 4 - o[2])), o),
)


def split(a):
    hi = a.astype(BF16)
    lo = (a - hi.astype(F32)).astype(BF16)
    return hi, lo


def dot3(a, b, dims):
    ah, al = a
    bh, bl = b
    dot = functools.partial(
        lax.dot_general, dimension_numbers=dims, preferred_element_type=F32
    )
    return dot(ah, bh) + (dot(ah, bl) + dot(al, bh))


def roll(x, shift, axis):
    return pltpu.roll(x, shift % x.shape[axis], axis)


def shifted(row, amount):
    for bit in range(5):
        flag = ((amount >> bit) & 1) == 1
        row = jnp.where(flag, roll(row, 1 << bit, 1), row)
    return row


def staircase(row, start):
    eight = jnp.broadcast_to(row, (8, row.shape[1]))
    eight = pltpu.roll(eight, 0, 1, stride=1, stride_axis=0)
    return jnp.concatenate([roll(eight, start + 8 * k, 1) for k in range(L // 8)], axis=0)


def band_blocks(row, amount):
    row = shifted(row, amount + 12)
    wide = jnp.concatenate([row, jnp.zeros((1, 2 * L), F32)], axis=1)
    return staircase(wide, 86)


def y_block(row):
    full = staircase(row, 121)
    rows = lax.broadcasted_iota(jnp.int32, (L, L), 0) // YDIM
    cols = lax.broadcasted_iota(jnp.int32, (L, L), 1) // YDIM
    return jnp.where(rows == cols, full, 0.0)


def swap_slab(x):
    rows = x.shape[0]
    x = x.reshape(rows // TILE, TILE, L)
    sub = lax.broadcasted_iota(jnp.int32, x.shape, 1)
    lane = lax.broadcasted_iota(jnp.int32, x.shape, 2) // YDIM
    for bit in (4, 2, 1):
        s_bit = (sub // bit) % 2
        same = s_bit == (lane // bit) % 2
        up = roll(roll(x, -bit, 1), YDIM * bit, 2)
        down = up if bit == 4 else roll(roll(x, bit, 1), -YDIM * bit, 2)
        x = jnp.where(same, x, jnp.where(s_bit == 0, up, down))
    return x.reshape(rows, L)


def taps(long_ref, short_ref, detect_ref, rows):
    rows[...] = jnp.zeros_like(rows)
    rows[0:1, 0 : long_ref.shape[1]] = long_ref[...]
    rows[1:3, 0 : short_ref.shape[2]] = short_ref[0]
    value = rows[...]
    value = value / jnp.maximum(jnp.sum(value, axis=1, keepdims=True), 1e-30)
    along, across, second = value[0:1], roll(value[1:2], 23, 1), value[2:3]
    is_first = detect_ref[0, 0] == 0
    offset = detect_ref[0, 1]
    first = jnp.where(is_first, along, across)
    third = jnp.where(is_first, across, along)
    return (
        (first, jnp.where(is_first, offset, 0)),
        second,
        (third, jnp.where(is_first, 0, offset)),
    )


def store_pair(ref, rows, cols, value):
    hi, lo = split(value)
    ref[0, rows, cols] = hi
    ref[1, rows, cols] = lo


def fill_rows(ref, blocks):
    zero = jnp.zeros((L, L), BF16)
    for part in range(2):
        ref[part, 0:L, 3 * L : 4 * L] = zero
        ref[part, L : 2 * L, 0:L] = zero
    store_pair(ref, slice(0, L), slice(0, 3 * L), blocks)
    store_pair(ref, slice(L, 2 * L), slice(L, 4 * L), blocks)


def fill_cols(ref, blocks):
    zero = jnp.zeros((L, L), BF16)
    left, here, right = (blocks[:, k * L : (k + 1) * L] for k in range(3))
    for part in range(2):
        ref[part, 0:L, L : 2 * L] = zero
        ref[part, 3 * L : 4 * L, 0:L] = zero
    for col in range(2):
        for row, value in enumerate((right, here, left)):
            store_pair(
                ref,
                slice((row + col) * L, (row + col + 1) * L),
                slice(col * L, (col + 1) * L),
                value,
            )


def fill_core(ref, blocks):
    near = roll(blocks, -EDGE, 1)[:, 0 : 2 * L]
    for part, value in enumerate(split(near)):
        ref[part * L : (part + 1) * L, :] = value


def store_lines(ref, rows, value):
    hi, lo = split(value)
    ref[rows, 0:L] = hi
    ref[rows, L : 2 * L] = lo


def correlate(core, lines, block):
    window = lines[pl.ds(pl.multiple_of(block * L, L), 2 * L), :]
    full = lax.dot_general(core[...], window, NN, preferred_element_type=F32)
    return full[0:L, 0:L] + (full[0:L, L : 2 * L] + full[L : 2 * L, 0:L])


HALVES = ((0, slice(L, 4 * L), slice(0, 3 * L)), (1, slice(0, 3 * L), slice(L, 4 * L)))


def kernel(
    est_hbm, views_hbm, long_hbm, short_hbm, detect_hbm, out_ref,
    est_ref, views_ref, long_ref, short_ref, detect_ref,
    rows, zrow, zcol, xcore, xtcore, views_t,
    send1, recv1, send2, recv2, lines, ratio, turned, corr, pair, part, final,
    isem, ssem, rsem, pair_ssem, pair_rsem, part_ssem, part_rsem,
    chip_ssem, chip_rsem, core_ssem, core_rsem,
):
    v = lax.axis_index("view")
    q = lax.axis_index("pencil")
    x, z, yh = q % 4, (q // 4) % 8, q // 32

    def pencil(off):
        a, b, c = off
        return (((yh + a) % 2) * 8 + (z + b) % 8) * 4 + (x + c) % 4

    barrier = pltpu.get_barrier_semaphore()
    for off in OFFSETS:
        pl.semaphore_signal(barrier, inc=1, device_id=(v, pencil(off)), device_id_type=MESH)
    core, chip = v % 2, v // 2
    partner = (chip * 2 + (1 - core), q)
    chips = [(3 - chip) % CHIPS, (chip + 2) % CHIPS, (5 - chip) % CHIPS]
    pl.semaphore_signal(barrier, inc=1, device_id=partner, device_id_type=MESH)
    for other in chips:
        pl.semaphore_signal(
            barrier, inc=1, device_id=(other * 2 + core, q), device_id_type=MESH
        )

    loads = [
        pltpu.make_async_copy(src, dst, isem.at[k])
        for k, (src, dst) in enumerate(
            (
                (long_hbm, long_ref),
                (short_hbm, short_ref),
                (detect_hbm, detect_ref),
                (est_hbm, est_ref),
                (views_hbm, views_ref),
            )
        )
    ]
    for load in loads:
        load.start()
    for load in loads[:3]:
        load.wait()

    (first, first_shift), second, (third, third_shift) = taps(
        long_ref, short_ref, detect_ref, rows
    )
    yb = y_block(second)
    zb = band_blocks(third, third_shift)
    fill_rows(zrow, zb)

    loads[3].wait()
    field = dot3(split(yb), split(est_ref[...]), NN)
    fh, fl = split(field)
    for half, cols, window in HALVES:
        send1[half * 256 : (half + 1) * 256, :] = dot3(
            (zrow[0, :, cols], zrow[1, :, cols]), (fh[:, window], fl[:, window]), NT
        )

    pl.semaphore_wait(barrier, PENCILS - 1 + CHIPS)

    def exchange(src, dst, k, far):
        mine = pl.ds(pl.multiple_of(q * TILE, TILE), TILE)
        for off in OFFSETS:
            if off[0] != far:
                continue
            peer = pencil(off)
            pltpu.make_async_remote_copy(
                src_ref=src.at[pl.ds(pl.multiple_of(peer * TILE, TILE), TILE), :],
                dst_ref=dst.at[mine, :],
                send_sem=ssem.at[2 * k + far],
                recv_sem=rsem.at[2 * k + far],
                device_id=(v, peer),
                device_id_type=MESH,
            ).start()
        if not far:
            dst[mine, :] = src[mine, :]

    def count(far):
        return pl.ds(0, (PENCILS // 2 - 1 + far) * TILE)

    def arrived(dst, k, far):
        view = dst.at[count(far), :]
        pltpu.make_async_copy(view, view, rsem.at[2 * k + far]).wait()

    def sent(src, k):
        for far in range(2):
            view = src.at[count(far), :]
            pltpu.make_async_copy(view, view, ssem.at[2 * k + far]).wait()

    def half_rows(half):
        return pl.ds(pl.multiple_of(half * 2 * L, 2 * L), 2 * L)

    planes = (yh, (yh + 1) % 2)

    for far in (1, 0):
        exchange(send1, recv1, 0, far)
    xb = band_blocks(first, first_shift)
    fill_core(xcore, xb)
    fill_core(
        xtcore,
        jnp.concatenate([xb[:, k * L : (k + 1) * L].T for k in (2, 1, 0)], axis=1),
    )
    fill_cols(zcol, zb)
    ytb = split(yb.T)
    margin = jnp.zeros((EDGE, 2 * L), BF16)
    for ref in (lines, ratio):
        ref[0:EDGE, :] = margin
        ref[EDGE + N :, :] = margin
    loads[4].wait()
    views_t[...] = views_ref[...].T

    def inner(start, size):
        return pl.ds(pl.multiple_of(EDGE + start, EDGE), size)

    def arrive(far):
        arrived(recv1, 0, far)
        half = planes[far]
        store_lines(lines, inner(half * 2 * L, 2 * L), swap_slab(recv1[half_rows(half), :]))

    def divide(block):
        views = views_t[pl.ds(pl.multiple_of(block * L, L), L), :]
        store_lines(ratio, inner(block * L, L), views / correlate(xcore, lines, block))

    arrive(0)
    divide(3 * planes[0])
    arrive(1)
    for block in (3 * planes[1], 1, 2):
        divide(block)
    for far in (1, 0):
        half = planes[far]
        back = [correlate(xtcore, ratio, 2 * half + k) for k in range(2)]
        send2[half_rows(half), :] = swap_slab(jnp.concatenate(back, axis=0))
        exchange(send2, recv2, 1, far)
    for far in range(2):
        arrived(recv2, 1, far)
        part_ = dot3(ytb, split(recv2[half_rows(planes[far]), :]), NT)
        for k, value in enumerate(split(part_)):
            turned[k, planes[far]] = value

    def quarter(c, b):
        return pl.ds(pl.multiple_of((c * CHIPS + b) * YDIM, YDIM), YDIM)

    def remote(src, dst, sems, index, device):
        send = pltpu.make_async_remote_copy(
            src_ref=src,
            dst_ref=dst,
            send_sem=sems[0].at[index],
            recv_sem=sems[1].at[index],
            device_id=device,
            device_id_type=MESH,
        )
        send.start()
        return send

    order = chips + [chip]
    same_core = [(b * 2 + core, q) for b in chips]
    bh, bl = (jnp.concatenate([turned[k, 0], turned[k, 1]], axis=1) for k in range(2))
    halves = {}
    for c, (_, rows_, window) in enumerate(HALVES):
        corr[c] = dot3(
            (bh[:, window], bl[:, window]), (zcol[0, rows_, :], zcol[1, rows_, :]), NN
        )
        for k, b in enumerate(order):
            halves[c, k] = remote(
                corr.at[c, quarter(1 - core, b), :], pair.at[c, b],
                (pair_ssem, pair_rsem), c * CHIPS + k, partner,
            )
    quarters = {}
    for c in range(CHUNKS):
        for k, b in enumerate(order):
            halves[c, k].wait_recv()
            pair[c, b] = pair[c, b] * corr[c, quarter(core, b), :]
            if k < CHIPS - 1:
                quarters[c, k] = remote(
                    pair.at[c, b], part.at[c, k],
                    (part_ssem, part_rsem), c * CHIPS + k, same_core[k],
                )
    gathers, locals_, relays = {}, [], []
    mine = quarter(core, chip)
    for c in range(CHUNKS):
        cols = pl.ds(c * HALF, HALF)
        for k in range(CHIPS - 1):
            quarters[c, k].wait_recv()
        own = est_ref[mine, c * HALF : (c + 1) * HALF] * pair[c, chip]
        final[c] = (own * part[c, 0]) * (part[c, 1] * part[c, 2])
        target = out_ref.at[mine, cols]
        for k in range(CHIPS - 1):
            gathers[c, k] = remote(
                final.at[c], target, (chip_ssem, chip_rsem), c * CHIPS + k, same_core[k]
            )
        relays.append(
            remote(final.at[c], target, (core_ssem, core_rsem), c * CHIPS + CHIPS - 1, partner)
        )
        local = pltpu.make_async_copy(final.at[c], target, isem.at[c])
        local.start()
        locals_.append(local)
    for c in range(CHUNKS):
        for k in (2, 1, 0):
            gathers[c, k].wait_recv()
            where = out_ref.at[quarter(core, chips[k]), pl.ds(c * HALF, HALF)]
            relays.append(remote(where, where, (core_ssem, core_rsem), c * CHIPS + k, partner))
    sent(send1, 0)
    sent(send2, 1)
    for sends in (halves, quarters, gathers):
        for send in sends.values():
            send.wait_send()
    for send in relays + locals_:
        send.wait()


def per_device(estimate, views_data, psf_long, psf_short, detection):
    raw = pl.BlockSpec(memory_space=pl.ANY)
    dma = pltpu.SemaphoreType.DMA
    updated = pl.pallas_call(
        kernel,
        out_shape=jax.ShapeDtypeStruct((L, N), F32),
        in_specs=[raw] * 5,
        out_specs=raw,
        scratch_shapes=[
            pltpu.VMEM((L, N), F32),
            pltpu.VMEM((L, N), F32),
            pltpu.VMEM(psf_long.shape, F32),
            pltpu.VMEM(psf_short.shape, F32),
            pltpu.SMEM(detection.shape, jnp.int32),
            pltpu.VMEM((8, L), F32),
            pltpu.VMEM((2, 2 * L, 4 * L), BF16),
            pltpu.VMEM((2, 4 * L, 2 * L), BF16),
            pltpu.VMEM((2 * L, 2 * L), BF16),
            pltpu.VMEM((2 * L, 2 * L), BF16),
            pltpu.VMEM((N, L), F32),
            pltpu.VMEM((N, L), F32),
            pltpu.VMEM((N, L), F32),
            pltpu.VMEM((N, L), F32),
            pltpu.VMEM((N, L), F32),
            pltpu.VMEM((N + 2 * EDGE, 2 * L), BF16),
            pltpu.VMEM((N + 2 * EDGE, 2 * L), BF16),
            pltpu.VMEM((2, 2, L, 2 * L), BF16),
            pltpu.VMEM((CHUNKS, L, HALF), F32),
            pltpu.VMEM((CHUNKS, CHIPS, YDIM, HALF), F32),
            pltpu.VMEM((CHUNKS, CHIPS - 1, YDIM, HALF), F32),
            pltpu.VMEM((CHUNKS, YDIM, HALF), F32),
            dma((5,)), dma((4,)), dma((4,)),
            *[dma((CHUNKS * CHIPS,))] * 8,
        ],
        compiler_params=pltpu.CompilerParams(
            collective_id=0, has_side_effects=True, vmem_limit_bytes=32 << 20
        ),
    )(
        *(
            pltpu.with_memory_space_constraint(a, pltpu.HBM)
            for a in (
                estimate.reshape(L, N),
                views_data.reshape(L, N),
                psf_long,
                psf_short,
                detection,
            )
        )
    )
    return updated.reshape(estimate.shape)


def solution(mesh):
    return jax.shard_map(
        per_device,
        mesh=mesh,
        in_specs=(
            P("pencil", None, None),
            P("view", "pencil", None, None),
            P("view", None),
            P("view", None, None),
            P("view", None),
        ),
        out_specs=P("pencil", None, None),
        check_vma=False,
    )
```

```python
import functools

import jax
import jax.numpy as jnp
from jax import lax
from jax.experimental import pallas as pl
from jax.experimental.pallas import tpu as pltpu
from jax.sharding import PartitionSpec as P

F32 = jnp.float32
BF16 = jnp.bfloat16
MESH = pl.DeviceIdType.MESH

VIEWS = 8
CHIPS = 4
PENCILS = 64
TILE = 8
N = 512
CHUNKS = 2
HALF = N // CHUNKS
L = 128
EDGE = 64
YDIM = 16

NN = (((1,), (0,)), ((), ()))
NT = (((1,), (1,)), ((), ()))

OFFSETS = sorted(
    ((a, b, c) for a in range(2) for b in range(8) for c in range(4) if a + b + c),
    key=lambda o: (-(4 * o[0] + min(o[1], 8 - o[1]) + min(o[2], 4 - o[2])), o),
)


def split(a):
    hi = a.astype(BF16)
    lo = (a - hi.astype(F32)).astype(BF16)
    return hi, lo


def dot3(a, b, dims):
    ah, al = a
    bh, bl = b
    dot = functools.partial(
        lax.dot_general, dimension_numbers=dims, preferred_element_type=F32
    )
    return dot(ah, bh) + (dot(ah, bl) + dot(al, bh))


def roll(x, shift, axis):
    return pltpu.roll(x, shift % x.shape[axis], axis)


def shifted(row, amount):
    for bit in range(5):
        flag = ((amount >> bit) & 1) == 1
        row = jnp.where(flag, roll(row, 1 << bit, 1), row)
    return row


def staircase(row, start):
    eight = jnp.broadcast_to(row, (8, row.shape[1]))
    eight = pltpu.roll(eight, 0, 1, stride=1, stride_axis=0)
    return jnp.concatenate([roll(eight, start + 8 * k, 1) for k in range(L // 8)], axis=0)


def band_blocks(row, amount):
    row = shifted(row, amount + 12)
    wide = jnp.concatenate([row, jnp.zeros((1, 2 * L), F32)], axis=1)
    return staircase(wide, 86)


def y_block(row):
    full = staircase(row, 121)
    rows = lax.broadcasted_iota(jnp.int32, (L, L), 0) // YDIM
    cols = lax.broadcasted_iota(jnp.int32, (L, L), 1) // YDIM
    return jnp.where(rows == cols, full, 0.0)


def swap_slab(x):
    rows = x.shape[0]
    x = x.reshape(rows // TILE, TILE, L)
    sub = lax.broadcasted_iota(jnp.int32, x.shape, 1)
    lane = lax.broadcasted_iota(jnp.int32, x.shape, 2) // YDIM
    for bit in (4, 2, 1):
        s_bit = (sub // bit) % 2
        same = s_bit == (lane // bit) % 2
        up = roll(roll(x, -bit, 1), YDIM * bit, 2)
        down = up if bit == 4 else roll(roll(x, bit, 1), -YDIM * bit, 2)
        x = jnp.where(same, x, jnp.where(s_bit == 0, up, down))
    return x.reshape(rows, L)


def taps(long_ref, short_ref, detect_ref, rows):
    rows[...] = jnp.zeros_like(rows)
    rows[0:1, 0 : long_ref.shape[1]] = long_ref[...]
    rows[1:3, 0 : short_ref.shape[2]] = short_ref[0]
    value = rows[...]
    value = value / jnp.maximum(jnp.sum(value, axis=1, keepdims=True), 1e-30)
    along, across, second = value[0:1], roll(value[1:2], 23, 1), value[2:3]
    is_first = detect_ref[0, 0] == 0
    offset = detect_ref[0, 1]
    first = jnp.where(is_first, along, across)
    third = jnp.where(is_first, across, along)
    return (
        (first, jnp.where(is_first, offset, 0)),
        second,
        (third, jnp.where(is_first, 0, offset)),
    )


def store_pair(ref, rows, cols, value):
    hi, lo = split(value)
    ref[0, rows, cols] = hi
    ref[1, rows, cols] = lo


def fill_rows(ref, blocks):
    zero = jnp.zeros((L, L), BF16)
    for part in range(2):
        ref[part, 0:L, 3 * L : 4 * L] = zero
        ref[part, L : 2 * L, 0:L] = zero
    store_pair(ref, slice(0, L), slice(0, 3 * L), blocks)
    store_pair(ref, slice(L, 2 * L), slice(L, 4 * L), blocks)


def fill_cols(ref, blocks):
    zero = jnp.zeros((L, L), BF16)
    left, here, right = (blocks[:, k * L : (k + 1) * L] for k in range(3))
    for part in range(2):
        ref[part, 0:L, L : 2 * L] = zero
        ref[part, 3 * L : 4 * L, 0:L] = zero
    for col in range(2):
        for row, value in enumerate((right, here, left)):
            store_pair(
                ref,
                slice((row + col) * L, (row + col + 1) * L),
                slice(col * L, (col + 1) * L),
                value,
            )


def fill_core(ref, blocks):
    near = roll(blocks, -EDGE, 1)[:, 0 : 2 * L]
    for part, value in enumerate(split(near)):
        ref[part * L : (part + 1) * L, :] = value


def store_lines(ref, rows, value):
    hi, lo = split(value)
    ref[rows, 0:L] = hi
    ref[rows, L : 2 * L] = lo


def correlate(core, lines, block):
    window = lines[pl.ds(pl.multiple_of(block * L, L), 2 * L), :]
    full = lax.dot_general(core[...], window, NN, preferred_element_type=F32)
    return full[0:L, 0:L] + (full[0:L, L : 2 * L] + full[L : 2 * L, 0:L])


HALVES = ((0, slice(L, 4 * L), slice(0, 3 * L)), (1, slice(0, 3 * L), slice(L, 4 * L)))


def kernel(
    est_hbm, views_hbm, long_hbm, short_hbm, detect_hbm, out_ref,
    est_ref, views_ref, long_ref, short_ref, detect_ref,
    rows, zrow, zcol, xcore, xtcore, views_t,
    send1, recv1, send2, recv2, lines, ratio, turned, corr, pair, part, final,
    isem, ssem, rsem, pair_ssem, pair_rsem, part_ssem, part_rsem,
    chip_ssem, chip_rsem, core_ssem, core_rsem,
):
    v = lax.axis_index("view")
    q = lax.axis_index("pencil")
    x, z, yh = q % 4, (q // 4) % 8, q // 32

    def pencil(off):
        a, b, c = off
        return (((yh + a) % 2) * 8 + (z + b) % 8) * 4 + (x + c) % 4

    barrier = pltpu.get_barrier_semaphore()
    for off in OFFSETS:
        pl.semaphore_signal(barrier, inc=1, device_id=(v, pencil(off)), device_id_type=MESH)
    core, chip = v % 2, v // 2
    partner = (chip * 2 + (1 - core), q)
    side = chip // 2
    chips = [3 - 3 * side, 2 - side, chip + 1 - 2 * (chip % 2)]
    pl.semaphore_signal(barrier, inc=1, device_id=partner, device_id_type=MESH)
    for other in chips:
        pl.semaphore_signal(
            barrier, inc=1, device_id=(other * 2 + core, q), device_id_type=MESH
        )

    loads = [
        pltpu.make_async_copy(src, dst, isem.at[k])
        for k, (src, dst) in enumerate(
            (
                (long_hbm, long_ref),
                (short_hbm, short_ref),
                (detect_hbm, detect_ref),
                (est_hbm, est_ref),
                (views_hbm, views_ref),
            )
        )
    ]
    for load in loads:
        load.start()
    for load in loads[:3]:
        load.wait()

    (first, first_shift), second, (third, third_shift) = taps(
        long_ref, short_ref, detect_ref, rows
    )
    yb = y_block(second)
    zb = band_blocks(third, third_shift)
    fill_rows(zrow, zb)

    loads[3].wait()
    field = dot3(split(yb), split(est_ref[...]), NN)
    fh, fl = split(field)
    for half, cols, window in HALVES:
        send1[half * 256 : (half + 1) * 256, :] = dot3(
            (zrow[0, :, cols], zrow[1, :, cols]), (fh[:, window], fl[:, window]), NT
        )

    pl.semaphore_wait(barrier, PENCILS - 1 + CHIPS)

    def exchange(src, dst, k, far):
        mine = pl.ds(pl.multiple_of(q * TILE, TILE), TILE)
        for off in OFFSETS:
            if off[0] != far:
                continue
            peer = pencil(off)
            pltpu.make_async_remote_copy(
                src_ref=src.at[pl.ds(pl.multiple_of(peer * TILE, TILE), TILE), :],
                dst_ref=dst.at[mine, :],
                send_sem=ssem.at[2 * k + far],
                recv_sem=rsem.at[2 * k + far],
                device_id=(v, peer),
                device_id_type=MESH,
            ).start()
        if not far:
            dst[mine, :] = src[mine, :]

    def count(far):
        return pl.ds(0, (PENCILS // 2 - 1 + far) * TILE)

    def arrived(dst, k, far):
        view = dst.at[count(far), :]
        pltpu.make_async_copy(view, view, rsem.at[2 * k + far]).wait()

    def sent(src, k):
        for far in range(2):
            view = src.at[count(far), :]
            pltpu.make_async_copy(view, view, ssem.at[2 * k + far]).wait()

    def half_rows(half):
        return pl.ds(pl.multiple_of(half * 2 * L, 2 * L), 2 * L)

    planes = (yh, (yh + 1) % 2)

    for far in (1, 0):
        exchange(send1, recv1, 0, far)
    xb = band_blocks(first, first_shift)
    fill_core(xcore, xb)
    fill_core(
        xtcore,
        jnp.concatenate([xb[:, k * L : (k + 1) * L].T for k in (2, 1, 0)], axis=1),
    )
    fill_cols(zcol, zb)
    ytb = split(yb.T)
    margin = jnp.zeros((EDGE, 2 * L), BF16)
    for ref in (lines, ratio):
        ref[0:EDGE, :] = margin
        ref[EDGE + N :, :] = margin
    loads[4].wait()
    views_t[...] = views_ref[...].T

    def inner(start, size):
        return pl.ds(pl.multiple_of(EDGE + start, EDGE), size)

    def arrive(far):
        arrived(recv1, 0, far)
        half = planes[far]
        store_lines(lines, inner(half * 2 * L, 2 * L), swap_slab(recv1[half_rows(half), :]))

    def divide(block):
        views = views_t[pl.ds(pl.multiple_of(block * L, L), L), :]
        store_lines(ratio, inner(block * L, L), views / correlate(xcore, lines, block))

    arrive(0)
    divide(3 * planes[0])
    arrive(1)
    for block in (3 * planes[1], 1, 2):
        divide(block)
    for far in (1, 0):
        half = planes[far]
        back = [correlate(xtcore, ratio, 2 * half + k) for k in range(2)]
        send2[half_rows(half), :] = swap_slab(jnp.concatenate(back, axis=0))
        exchange(send2, recv2, 1, far)
    for far in range(2):
        arrived(recv2, 1, far)
        part_ = dot3(ytb, split(recv2[half_rows(planes[far]), :]), NT)
        for k, value in enumerate(split(part_)):
            turned[k, planes[far]] = value

    def quarter(c, b):
        return pl.ds(pl.multiple_of((c * CHIPS + b) * YDIM, YDIM), YDIM)

    def remote(src, dst, sems, k, slot, device):
        return pltpu.make_async_remote_copy(
            src_ref=src,
            dst_ref=dst,
            send_sem=sems[0].at[k],
            recv_sem=sems[1].at[slot],
            device_id=device,
            device_id_type=MESH,
        )

    def push(*args):
        send = remote(*args)
        send.start()
        return send

    def place(c, b):
        return out_ref.at[quarter(core, b), pl.ds(c * HALF, HALF)]

    order = chips + [chip]
    same_core = [(b * 2 + core, q) for b in chips]
    bh, bl = (jnp.concatenate([turned[k, 0], turned[k, 1]], axis=1) for k in range(2))
    halves = {}
    for c, (_, rows_, window) in enumerate(HALVES):
        corr[c] = dot3(
            (bh[:, window], bl[:, window]), (zcol[0, rows_, :], zcol[1, rows_, :]), NN
        )
        for k, b in enumerate(order):
            halves[c, k] = push(
                corr.at[c, quarter(1 - core, b), :], pair.at[c, b],
                (pair_ssem, pair_rsem), c * CHIPS + k, c * CHIPS + k, partner,
            )
    quarters = {}
    for c in range(CHUNKS):
        for k, b in enumerate(order):
            halves[c, k].wait_recv()
            pair[c, b] = pair[c, b] * corr[c, quarter(core, b), :]
            if k < CHIPS - 1:
                quarters[c, k] = push(
                    pair.at[c, b], part.at[c, chip],
                    (part_ssem, part_rsem), c * CHIPS + k, c * CHIPS + chip, same_core[k],
                )
    gathers, locals_, relays = {}, [], []
    mine = quarter(core, chip)
    for c in range(CHUNKS):
        for b in chips:
            remote(
                pair.at[c, b], part.at[c, b],
                (part_ssem, part_rsem), c * CHIPS, c * CHIPS + b, partner,
            ).wait_recv()
        own = est_ref[mine, c * HALF : (c + 1) * HALF] * pair[c, chip]
        final[c] = (own * part[c, chips[0]]) * (part[c, chips[1]] * part[c, chips[2]])
        for k in range(CHIPS - 1):
            gathers[c, k] = push(
                final.at[c], place(c, chip),
                (chip_ssem, chip_rsem), c * CHIPS + k, c * CHIPS + chip, same_core[k],
            )
        relays.append(
            push(
                final.at[c], place(c, chip),
                (core_ssem, core_rsem), c * CHIPS + chip, c * CHIPS + chip, partner,
            )
        )
        local = pltpu.make_async_copy(final.at[c], place(c, chip), isem.at[c])
        local.start()
        locals_.append(local)
    for c in range(CHUNKS):
        for b in (chips[2], chips[1], chips[0]):
            remote(
                final.at[c], place(c, b),
                (chip_ssem, chip_rsem), c * CHIPS, c * CHIPS + b, partner,
            ).wait_recv()
            relays.append(
                push(
                    place(c, b), place(c, b),
                    (core_ssem, core_rsem), c * CHIPS + b, c * CHIPS + b, partner,
                )
            )
    sent(send1, 0)
    sent(send2, 1)
    for sends in (halves, quarters, gathers):
        for send in sends.values():
            send.wait_send()
    for send in relays + locals_:
        send.wait()


def per_device(estimate, views_data, psf_long, psf_short, detection):
    raw = pl.BlockSpec(memory_space=pl.ANY)
    dma = pltpu.SemaphoreType.DMA
    updated = pl.pallas_call(
        kernel,
        out_shape=jax.ShapeDtypeStruct((L, N), F32),
        in_specs=[raw] * 5,
        out_specs=raw,
        scratch_shapes=[
            pltpu.VMEM((L, N), F32),
            pltpu.VMEM((L, N), F32),
            pltpu.VMEM(psf_long.shape, F32),
            pltpu.VMEM(psf_short.shape, F32),
            pltpu.SMEM(detection.shape, jnp.int32),
            pltpu.VMEM((8, L), F32),
            pltpu.VMEM((2, 2 * L, 4 * L), BF16),
            pltpu.VMEM((2, 4 * L, 2 * L), BF16),
            pltpu.VMEM((2 * L, 2 * L), BF16),
            pltpu.VMEM((2 * L, 2 * L), BF16),
            pltpu.VMEM((N, L), F32),
            pltpu.VMEM((N, L), F32),
            pltpu.VMEM((N, L), F32),
            pltpu.VMEM((N, L), F32),
            pltpu.VMEM((N, L), F32),
            pltpu.VMEM((N + 2 * EDGE, 2 * L), BF16),
            pltpu.VMEM((N + 2 * EDGE, 2 * L), BF16),
            pltpu.VMEM((2, 2, L, 2 * L), BF16),
            pltpu.VMEM((CHUNKS, L, HALF), F32),
            pltpu.VMEM((CHUNKS, CHIPS, YDIM, HALF), F32),
            pltpu.VMEM((CHUNKS, CHIPS, YDIM, HALF), F32),
            pltpu.VMEM((CHUNKS, YDIM, HALF), F32),
            dma((5,)), dma((4,)), dma((4,)),
            *[dma((CHUNKS * CHIPS,))] * 8,
        ],
        compiler_params=pltpu.CompilerParams(
            collective_id=0, has_side_effects=True, vmem_limit_bytes=32 << 20
        ),
    )(
        *(
            pltpu.with_memory_space_constraint(a, pltpu.HBM)
            for a in (
                estimate.reshape(L, N),
                views_data.reshape(L, N),
                psf_long,
                psf_short,
                detection,
            )
        )
    )
    return updated.reshape(estimate.shape)


def solution(mesh):
    return jax.shard_map(
        per_device,
        mesh=mesh,
        in_specs=(
            P("pencil", None, None),
            P("view", "pencil", None, None),
            P("view", None),
            P("view", None, None),
            P("view", None),
        ),
        out_specs=P("pencil", None, None),
        check_vma=False,
    )
```

```python
import functools

import jax
import jax.numpy as jnp
from jax import lax
from jax.experimental import pallas as pl
from jax.experimental.pallas import tpu as pltpu
from jax.sharding import PartitionSpec as P

F32 = jnp.float32
BF16 = jnp.bfloat16
MESH = pl.DeviceIdType.MESH

VIEWS = 8
CHIPS = 4
PENCILS = 64
TILE = 8
N = 512
CHUNKS = 4
HALF = N // CHUNKS
L = 128
EDGE = 64
YDIM = 16

NN = (((1,), (0,)), ((), ()))
NT = (((1,), (1,)), ((), ()))

OFFSETS = sorted(
    ((a, b, c) for a in range(2) for b in range(8) for c in range(4) if a + b + c),
    key=lambda o: (-(4 * o[0] + min(o[1], 8 - o[1]) + min(o[2], 4 - o[2])), o),
)


def split(a):
    hi = a.astype(BF16)
    lo = (a - hi.astype(F32)).astype(BF16)
    return hi, lo


def dot3(a, b, dims):
    ah, al = a
    bh, bl = b
    dot = functools.partial(
        lax.dot_general, dimension_numbers=dims, preferred_element_type=F32
    )
    return dot(ah, bh) + (dot(ah, bl) + dot(al, bh))


def roll(x, shift, axis):
    return pltpu.roll(x, shift % x.shape[axis], axis)


def shifted(row, amount):
    for bit in range(5):
        flag = ((amount >> bit) & 1) == 1
        row = jnp.where(flag, roll(row, 1 << bit, 1), row)
    return row


def staircase(row, start):
    eight = jnp.broadcast_to(row, (8, row.shape[1]))
    eight = pltpu.roll(eight, 0, 1, stride=1, stride_axis=0)
    return jnp.concatenate([roll(eight, start + 8 * k, 1) for k in range(L // 8)], axis=0)


def band_blocks(row, amount):
    row = shifted(row, amount + 12)
    wide = jnp.concatenate([row, jnp.zeros((1, 2 * L), F32)], axis=1)
    return staircase(wide, 86)


def y_block(row):
    full = staircase(row, 121)
    rows = lax.broadcasted_iota(jnp.int32, (L, L), 0) // YDIM
    cols = lax.broadcasted_iota(jnp.int32, (L, L), 1) // YDIM
    return jnp.where(rows == cols, full, 0.0)


def swap_slab(x):
    rows = x.shape[0]
    x = x.reshape(rows // TILE, TILE, L)
    sub = lax.broadcasted_iota(jnp.int32, x.shape, 1)
    lane = lax.broadcasted_iota(jnp.int32, x.shape, 2) // YDIM
    for bit in (4, 2, 1):
        s_bit = (sub // bit) % 2
        same = s_bit == (lane // bit) % 2
        up = roll(roll(x, -bit, 1), YDIM * bit, 2)
        down = up if bit == 4 else roll(roll(x, bit, 1), -YDIM * bit, 2)
        x = jnp.where(same, x, jnp.where(s_bit == 0, up, down))
    return x.reshape(rows, L)


def taps(long_ref, short_ref, detect_ref, rows):
    rows[...] = jnp.zeros_like(rows)
    rows[0:1, 0 : long_ref.shape[1]] = long_ref[...]
    rows[1:3, 0 : short_ref.shape[2]] = short_ref[0]
    value = rows[...]
    value = value / jnp.maximum(jnp.sum(value, axis=1, keepdims=True), 1e-30)
    along, across, second = value[0:1], roll(value[1:2], 23, 1), value[2:3]
    is_first = detect_ref[0, 0] == 0
    offset = detect_ref[0, 1]
    first = jnp.where(is_first, along, across)
    third = jnp.where(is_first, across, along)
    return (
        (first, jnp.where(is_first, offset, 0)),
        second,
        (third, jnp.where(is_first, 0, offset)),
    )


def store_pair(ref, rows, cols, value):
    hi, lo = split(value)
    ref[0, rows, cols] = hi
    ref[1, rows, cols] = lo


def fill_rows(ref, blocks):
    zero = jnp.zeros((L, L), BF16)
    for part in range(2):
        ref[part, 0:L, 3 * L : 4 * L] = zero
        ref[part, L : 2 * L, 0:L] = zero
    store_pair(ref, slice(0, L), slice(0, 3 * L), blocks)
    store_pair(ref, slice(L, 2 * L), slice(L, 4 * L), blocks)


def fill_cols(ref, blocks):
    zero = jnp.zeros((L, L), BF16)
    left, here, right = (blocks[:, k * L : (k + 1) * L] for k in range(3))
    for part in range(2):
        ref[part, 0:L, L : 2 * L] = zero
        ref[part, 3 * L : 4 * L, 0:L] = zero
    for col in range(2):
        for row, value in enumerate((right, here, left)):
            store_pair(
                ref,
                slice((row + col) * L, (row + col + 1) * L),
                slice(col * L, (col + 1) * L),
                value,
            )


def fill_core(ref, blocks):
    near = roll(blocks, -EDGE, 1)[:, 0 : 2 * L]
    for part, value in enumerate(split(near)):
        ref[part * L : (part + 1) * L, :] = value


def store_lines(ref, rows, value):
    hi, lo = split(value)
    ref[rows, 0:L] = hi
    ref[rows, L : 2 * L] = lo


def correlate(core, lines, block):
    window = lines[pl.ds(pl.multiple_of(block * L, L), 2 * L), :]
    full = lax.dot_general(core[...], window, NN, preferred_element_type=F32)
    return full[0:L, 0:L] + (full[0:L, L : 2 * L] + full[L : 2 * L, 0:L])


HALVES = ((0, slice(L, 4 * L), slice(0, 3 * L)), (1, slice(0, 3 * L), slice(L, 4 * L)))


def kernel(
    est_hbm, views_hbm, long_hbm, short_hbm, detect_hbm, out_ref,
    est_ref, views_ref, long_ref, short_ref, detect_ref,
    rows, zrow, zcol, xcore, xtcore, views_t,
    send1, recv1, send2, recv2, lines, ratio, turned, corr, pair, part, final,
    isem, ssem, rsem, pair_ssem, pair_rsem, part_ssem, part_rsem,
    chip_ssem, chip_rsem, core_ssem, core_rsem,
):
    v = lax.axis_index("view")
    q = lax.axis_index("pencil")
    x, z, yh = q % 4, (q // 4) % 8, q // 32

    def pencil(off):
        a, b, c = off
        return (((yh + a) % 2) * 8 + (z + b) % 8) * 4 + (x + c) % 4

    barrier = pltpu.get_barrier_semaphore()
    for off in OFFSETS:
        pl.semaphore_signal(barrier, inc=1, device_id=(v, pencil(off)), device_id_type=MESH)
    core, chip = v % 2, v // 2
    partner = (chip * 2 + (1 - core), q)
    chips = [(3 - chip) % CHIPS, (chip + 2) % CHIPS, (5 - chip) % CHIPS]
    pl.semaphore_signal(barrier, inc=1, device_id=partner, device_id_type=MESH)
    for other in chips:
        pl.semaphore_signal(
            barrier, inc=1, device_id=(other * 2 + core, q), device_id_type=MESH
        )

    loads = [
        pltpu.make_async_copy(src, dst, isem.at[k])
        for k, (src, dst) in enumerate(
            (
                (long_hbm, long_ref),
                (short_hbm, short_ref),
                (detect_hbm, detect_ref),
                (est_hbm, est_ref),
                (views_hbm, views_ref),
            )
        )
    ]
    for load in loads:
        load.start()
    for load in loads[:3]:
        load.wait()

    (first, first_shift), second, (third, third_shift) = taps(
        long_ref, short_ref, detect_ref, rows
    )
    yb = y_block(second)
    zb = band_blocks(third, third_shift)
    fill_rows(zrow, zb)

    loads[3].wait()
    field = dot3(split(yb), split(est_ref[...]), NN)
    fh, fl = split(field)
    for half, cols, window in HALVES:
        send1[half * 256 : (half + 1) * 256, :] = dot3(
            (zrow[0, :, cols], zrow[1, :, cols]), (fh[:, window], fl[:, window]), NT
        )

    pl.semaphore_wait(barrier, PENCILS - 1 + CHIPS)

    def exchange(src, dst, k, far):
        mine = pl.ds(pl.multiple_of(q * TILE, TILE), TILE)
        for off in OFFSETS:
            if off[0] != far:
                continue
            peer = pencil(off)
            pltpu.make_async_remote_copy(
                src_ref=src.at[pl.ds(pl.multiple_of(peer * TILE, TILE), TILE), :],
                dst_ref=dst.at[mine, :],
                send_sem=ssem.at[2 * k + far],
                recv_sem=rsem.at[2 * k + far],
                device_id=(v, peer),
                device_id_type=MESH,
            ).start()
        if not far:
            dst[mine, :] = src[mine, :]

    def count(far):
        return pl.ds(0, (PENCILS // 2 - 1 + far) * TILE)

    def arrived(dst, k, far):
        view = dst.at[count(far), :]
        pltpu.make_async_copy(view, view, rsem.at[2 * k + far]).wait()

    def sent(src, k):
        for far in range(2):
            view = src.at[count(far), :]
            pltpu.make_async_copy(view, view, ssem.at[2 * k + far]).wait()

    def half_rows(half):
        return pl.ds(pl.multiple_of(half * 2 * L, 2 * L), 2 * L)

    planes = (yh, (yh + 1) % 2)

    for far in (1, 0):
        exchange(send1, recv1, 0, far)
    xb = band_blocks(first, first_shift)
    fill_core(xcore, xb)
    fill_core(
        xtcore,
        jnp.concatenate([xb[:, k * L : (k + 1) * L].T for k in (2, 1, 0)], axis=1),
    )
    fill_cols(zcol, zb)
    ytb = split(yb.T)
    margin = jnp.zeros((EDGE, 2 * L), BF16)
    for ref in (lines, ratio):
        ref[0:EDGE, :] = margin
        ref[EDGE + N :, :] = margin
    loads[4].wait()
    views_t[...] = views_ref[...].T

    def inner(start, size):
        return pl.ds(pl.multiple_of(EDGE + start, EDGE), size)

    def arrive(far):
        arrived(recv1, 0, far)
        half = planes[far]
        store_lines(lines, inner(half * 2 * L, 2 * L), swap_slab(recv1[half_rows(half), :]))

    def divide(block):
        views = views_t[pl.ds(pl.multiple_of(block * L, L), L), :]
        store_lines(ratio, inner(block * L, L), views / correlate(xcore, lines, block))

    arrive(0)
    divide(3 * planes[0])
    arrive(1)
    for block in (3 * planes[1], 1, 2):
        divide(block)
    for far in (1, 0):
        half = planes[far]
        back = [correlate(xtcore, ratio, 2 * half + k) for k in range(2)]
        send2[half_rows(half), :] = swap_slab(jnp.concatenate(back, axis=0))
        exchange(send2, recv2, 1, far)
    for far in range(2):
        arrived(recv2, 1, far)
        part_ = dot3(ytb, split(recv2[half_rows(planes[far]), :]), NT)
        for k, value in enumerate(split(part_)):
            turned[k, planes[far]] = value

    def quarter(c, b):
        return pl.ds(pl.multiple_of((c * CHIPS + b) * YDIM, YDIM), YDIM)

    def remote(src, dst, sems, index, device):
        send = pltpu.make_async_remote_copy(
            src_ref=src,
            dst_ref=dst,
            send_sem=sems[0].at[index],
            recv_sem=sems[1].at[index],
            device_id=device,
            device_id_type=MESH,
        )
        send.start()
        return send

    order = chips + [chip]
    same_core = [(b * 2 + core, q) for b in chips]
    bh, bl = (jnp.concatenate([turned[k, 0], turned[k, 1]], axis=1) for k in range(2))
    halves = {}
    for half, rows_, window in HALVES:
        both = dot3(
            (bh[:, window], bl[:, window]), (zcol[0, rows_, :], zcol[1, rows_, :]), NN
        )
        for c in (2 * half, 2 * half + 1):
            corr[c] = both[:, (c % 2) * HALF : (c % 2 + 1) * HALF]
            for k, b in enumerate(order):
                halves[c, k] = remote(
                    corr.at[c, quarter(1 - core, b), :], pair.at[c, b],
                    (pair_ssem, pair_rsem), c * CHIPS + k, partner,
                )
    quarters = {}
    for c in range(CHUNKS):
        for k, b in enumerate(order):
            halves[c, k].wait_recv()
            pair[c, b] = pair[c, b] * corr[c, quarter(core, b), :]
            if k < CHIPS - 1:
                quarters[c, k] = remote(
                    pair.at[c, b], part.at[c, k],
                    (part_ssem, part_rsem), c * CHIPS + k, same_core[k],
                )
    gathers, locals_, relays = {}, [], []
    mine = quarter(core, chip)
    for c in range(CHUNKS):
        cols = pl.ds(c * HALF, HALF)
        for k in range(CHIPS - 1):
            quarters[c, k].wait_recv()
        own = est_ref[mine, c * HALF : (c + 1) * HALF] * pair[c, chip]
        final[c] = (own * part[c, 0]) * (part[c, 1] * part[c, 2])
        target = out_ref.at[mine, cols]
        for k in range(CHIPS - 1):
            gathers[c, k] = remote(
                final.at[c], target, (chip_ssem, chip_rsem), c * CHIPS + k, same_core[k]
            )
        relays.append(
            remote(final.at[c], target, (core_ssem, core_rsem), c * CHIPS + CHIPS - 1, partner)
        )
        local = pltpu.make_async_copy(final.at[c], target, isem.at[c])
        local.start()
        locals_.append(local)
    for c in range(CHUNKS):
        for k in (2, 1, 0):
            gathers[c, k].wait_recv()
            where = out_ref.at[quarter(core, chips[k]), pl.ds(c * HALF, HALF)]
            relays.append(remote(where, where, (core_ssem, core_rsem), c * CHIPS + k, partner))
    sent(send1, 0)
    sent(send2, 1)
    for sends in (halves, quarters, gathers):
        for send in sends.values():
            send.wait_send()
    for send in relays + locals_:
        send.wait()


def per_device(estimate, views_data, psf_long, psf_short, detection):
    raw = pl.BlockSpec(memory_space=pl.ANY)
    dma = pltpu.SemaphoreType.DMA
    updated = pl.pallas_call(
        kernel,
        out_shape=jax.ShapeDtypeStruct((L, N), F32),
        in_specs=[raw] * 5,
        out_specs=raw,
        scratch_shapes=[
            pltpu.VMEM((L, N), F32),
            pltpu.VMEM((L, N), F32),
            pltpu.VMEM(psf_long.shape, F32),
            pltpu.VMEM(psf_short.shape, F32),
            pltpu.SMEM(detection.shape, jnp.int32),
            pltpu.VMEM((8, L), F32),
            pltpu.VMEM((2, 2 * L, 4 * L), BF16),
            pltpu.VMEM((2, 4 * L, 2 * L), BF16),
            pltpu.VMEM((2 * L, 2 * L), BF16),
            pltpu.VMEM((2 * L, 2 * L), BF16),
            pltpu.VMEM((N, L), F32),
            pltpu.VMEM((N, L), F32),
            pltpu.VMEM((N, L), F32),
            pltpu.VMEM((N, L), F32),
            pltpu.VMEM((N, L), F32),
            pltpu.VMEM((N + 2 * EDGE, 2 * L), BF16),
            pltpu.VMEM((N + 2 * EDGE, 2 * L), BF16),
            pltpu.VMEM((2, 2, L, 2 * L), BF16),
            pltpu.VMEM((CHUNKS, L, HALF), F32),
            pltpu.VMEM((CHUNKS, CHIPS, YDIM, HALF), F32),
            pltpu.VMEM((CHUNKS, CHIPS - 1, YDIM, HALF), F32),
            pltpu.VMEM((CHUNKS, YDIM, HALF), F32),
            dma((5,)), dma((4,)), dma((4,)),
            *[dma((CHUNKS * CHIPS,))] * 8,
        ],
        compiler_params=pltpu.CompilerParams(
            collective_id=0, has_side_effects=True, vmem_limit_bytes=32 << 20
        ),
    )(
        *(
            pltpu.with_memory_space_constraint(a, pltpu.HBM)
            for a in (
                estimate.reshape(L, N),
                views_data.reshape(L, N),
                psf_long,
                psf_short,
                detection,
            )
        )
    )
    return updated.reshape(estimate.shape)


def solution(mesh):
    return jax.shard_map(
        per_device,
        mesh=mesh,
        in_specs=(
            P("pencil", None, None),
            P("view", "pencil", None, None),
            P("view", None),
            P("view", None, None),
            P("view", None),
        ),
        out_specs=P("pencil", None, None),
        check_vma=False,
    )
```

```python
import functools

import jax
import jax.numpy as jnp
from jax import lax
from jax.experimental import pallas as pl
from jax.experimental.pallas import tpu as pltpu
from jax.sharding import PartitionSpec as P

F32 = jnp.float32
BF16 = jnp.bfloat16
MESH = pl.DeviceIdType.MESH

VIEWS = 8
CHIPS = 4
PENCILS = 64
TILE = 8
N = 512
CHUNKS = 1
HALF = N // CHUNKS
L = 128
EDGE = 64
YDIM = 16

NN = (((1,), (0,)), ((), ()))
NT = (((1,), (1,)), ((), ()))

OFFSETS = sorted(
    ((a, b, c) for a in range(2) for b in range(8) for c in range(4) if a + b + c),
    key=lambda o: (-(4 * o[0] + min(o[1], 8 - o[1]) + min(o[2], 4 - o[2])), o),
)


def split(a):
    hi = a.astype(BF16)
    lo = (a - hi.astype(F32)).astype(BF16)
    return hi, lo


def dot3(a, b, dims):
    ah, al = a
    bh, bl = b
    dot = functools.partial(
        lax.dot_general, dimension_numbers=dims, preferred_element_type=F32
    )
    return dot(ah, bh) + (dot(ah, bl) + dot(al, bh))


def roll(x, shift, axis):
    return pltpu.roll(x, shift % x.shape[axis], axis)


def shifted(row, amount):
    for bit in range(5):
        flag = ((amount >> bit) & 1) == 1
        row = jnp.where(flag, roll(row, 1 << bit, 1), row)
    return row


def staircase(row, start):
    eight = jnp.broadcast_to(row, (8, row.shape[1]))
    eight = pltpu.roll(eight, 0, 1, stride=1, stride_axis=0)
    return jnp.concatenate([roll(eight, start + 8 * k, 1) for k in range(L // 8)], axis=0)


def band_blocks(row, amount):
    row = shifted(row, amount + 12)
    wide = jnp.concatenate([row, jnp.zeros((1, 2 * L), F32)], axis=1)
    return staircase(wide, 86)


def y_block(row):
    full = staircase(row, 121)
    rows = lax.broadcasted_iota(jnp.int32, (L, L), 0) // YDIM
    cols = lax.broadcasted_iota(jnp.int32, (L, L), 1) // YDIM
    return jnp.where(rows == cols, full, 0.0)


def swap_slab(x):
    rows = x.shape[0]
    x = x.reshape(rows // TILE, TILE, L)
    sub = lax.broadcasted_iota(jnp.int32, x.shape, 1)
    lane = lax.broadcasted_iota(jnp.int32, x.shape, 2) // YDIM
    for bit in (4, 2, 1):
        s_bit = (sub // bit) % 2
        same = s_bit == (lane // bit) % 2
        up = roll(roll(x, -bit, 1), YDIM * bit, 2)
        down = up if bit == 4 else roll(roll(x, bit, 1), -YDIM * bit, 2)
        x = jnp.where(same, x, jnp.where(s_bit == 0, up, down))
    return x.reshape(rows, L)


def taps(long_ref, short_ref, detect_ref, rows):
    rows[...] = jnp.zeros_like(rows)
    rows[0:1, 0 : long_ref.shape[1]] = long_ref[...]
    rows[1:3, 0 : short_ref.shape[2]] = short_ref[0]
    value = rows[...]
    value = value / jnp.maximum(jnp.sum(value, axis=1, keepdims=True), 1e-30)
    along, across, second = value[0:1], roll(value[1:2], 23, 1), value[2:3]
    is_first = detect_ref[0, 0] == 0
    offset = detect_ref[0, 1]
    first = jnp.where(is_first, along, across)
    third = jnp.where(is_first, across, along)
    return (
        (first, jnp.where(is_first, offset, 0)),
        second,
        (third, jnp.where(is_first, 0, offset)),
    )


def store_pair(ref, rows, cols, value):
    hi, lo = split(value)
    ref[0, rows, cols] = hi
    ref[1, rows, cols] = lo


def fill_rows(ref, blocks):
    zero = jnp.zeros((L, L), BF16)
    for part in range(2):
        ref[part, 0:L, 3 * L : 4 * L] = zero
        ref[part, L : 2 * L, 0:L] = zero
    store_pair(ref, slice(0, L), slice(0, 3 * L), blocks)
    store_pair(ref, slice(L, 2 * L), slice(L, 4 * L), blocks)


def fill_cols(ref, blocks):
    zero = jnp.zeros((L, L), BF16)
    left, here, right = (blocks[:, k * L : (k + 1) * L] for k in range(3))
    for part in range(2):
        ref[part, 0:L, L : 2 * L] = zero
        ref[part, 3 * L : 4 * L, 0:L] = zero
    for col in range(2):
        for row, value in enumerate((right, here, left)):
            store_pair(
                ref,
                slice((row + col) * L, (row + col + 1) * L),
                slice(col * L, (col + 1) * L),
                value,
            )


def fill_core(ref, blocks):
    near = roll(blocks, -EDGE, 1)[:, 0 : 2 * L]
    for part, value in enumerate(split(near)):
        ref[part * L : (part + 1) * L, :] = value


def store_lines(ref, rows, value):
    hi, lo = split(value)
    ref[rows, 0:L] = hi
    ref[rows, L : 2 * L] = lo


def correlate(core, lines, block):
    window = lines[pl.ds(pl.multiple_of(block * L, L), 2 * L), :]
    full = lax.dot_general(core[...], window, NN, preferred_element_type=F32)
    return full[0:L, 0:L] + (full[0:L, L : 2 * L] + full[L : 2 * L, 0:L])


HALVES = ((0, slice(L, 4 * L), slice(0, 3 * L)), (1, slice(0, 3 * L), slice(L, 4 * L)))


def kernel(
    est_hbm, views_hbm, long_hbm, short_hbm, detect_hbm, out_ref,
    est_ref, views_ref, long_ref, short_ref, detect_ref,
    rows, zrow, zcol, xcore, xtcore, views_t,
    send1, recv1, send2, recv2, lines, ratio, turned, corr, pair, part, final,
    isem, ssem, rsem, pair_ssem, pair_rsem, part_ssem, part_rsem,
    chip_ssem, chip_rsem, core_ssem, core_rsem,
):
    v = lax.axis_index("view")
    q = lax.axis_index("pencil")
    x, z, yh = q % 4, (q // 4) % 8, q // 32

    def pencil(off):
        a, b, c = off
        return (((yh + a) % 2) * 8 + (z + b) % 8) * 4 + (x + c) % 4

    barrier = pltpu.get_barrier_semaphore()
    for off in OFFSETS:
        pl.semaphore_signal(barrier, inc=1, device_id=(v, pencil(off)), device_id_type=MESH)
    core, chip = v % 2, v // 2
    partner = (chip * 2 + (1 - core), q)
    chips = [(3 - chip) % CHIPS, (chip + 2) % CHIPS, (5 - chip) % CHIPS]
    pl.semaphore_signal(barrier, inc=1, device_id=partner, device_id_type=MESH)
    for other in chips:
        pl.semaphore_signal(
            barrier, inc=1, device_id=(other * 2 + core, q), device_id_type=MESH
        )

    loads = [
        pltpu.make_async_copy(src, dst, isem.at[k])
        for k, (src, dst) in enumerate(
            (
                (long_hbm, long_ref),
                (short_hbm, short_ref),
                (detect_hbm, detect_ref),
                (est_hbm, est_ref),
                (views_hbm, views_ref),
            )
        )
    ]
    for load in loads:
        load.start()
    for load in loads[:3]:
        load.wait()

    (first, first_shift), second, (third, third_shift) = taps(
        long_ref, short_ref, detect_ref, rows
    )
    yb = y_block(second)
    zb = band_blocks(third, third_shift)
    fill_rows(zrow, zb)

    loads[3].wait()
    field = dot3(split(yb), split(est_ref[...]), NN)
    fh, fl = split(field)
    for half, cols, window in HALVES:
        send1[half * 256 : (half + 1) * 256, :] = dot3(
            (zrow[0, :, cols], zrow[1, :, cols]), (fh[:, window], fl[:, window]), NT
        )

    pl.semaphore_wait(barrier, PENCILS - 1 + CHIPS)

    def exchange(src, dst, k, far):
        mine = pl.ds(pl.multiple_of(q * TILE, TILE), TILE)
        for off in OFFSETS:
            if off[0] != far:
                continue
            peer = pencil(off)
            pltpu.make_async_remote_copy(
                src_ref=src.at[pl.ds(pl.multiple_of(peer * TILE, TILE), TILE), :],
                dst_ref=dst.at[mine, :],
                send_sem=ssem.at[2 * k + far],
                recv_sem=rsem.at[2 * k + far],
                device_id=(v, peer),
                device_id_type=MESH,
            ).start()
        if not far:
            dst[mine, :] = src[mine, :]

    def count(far):
        return pl.ds(0, (PENCILS // 2 - 1 + far) * TILE)

    def arrived(dst, k, far):
        view = dst.at[count(far), :]
        pltpu.make_async_copy(view, view, rsem.at[2 * k + far]).wait()

    def sent(src, k):
        for far in range(2):
            view = src.at[count(far), :]
            pltpu.make_async_copy(view, view, ssem.at[2 * k + far]).wait()

    def half_rows(half):
        return pl.ds(pl.multiple_of(half * 2 * L, 2 * L), 2 * L)

    planes = (yh, (yh + 1) % 2)

    for far in (1, 0):
        exchange(send1, recv1, 0, far)
    xb = band_blocks(first, first_shift)
    fill_core(xcore, xb)
    fill_core(
        xtcore,
        jnp.concatenate([xb[:, k * L : (k + 1) * L].T for k in (2, 1, 0)], axis=1),
    )
    fill_cols(zcol, zb)
    ytb = split(yb.T)
    margin = jnp.zeros((EDGE, 2 * L), BF16)
    for ref in (lines, ratio):
        ref[0:EDGE, :] = margin
        ref[EDGE + N :, :] = margin
    loads[4].wait()
    views_t[...] = views_ref[...].T

    def inner(start, size):
        return pl.ds(pl.multiple_of(EDGE + start, EDGE), size)

    def arrive(far):
        arrived(recv1, 0, far)
        half = planes[far]
        store_lines(lines, inner(half * 2 * L, 2 * L), swap_slab(recv1[half_rows(half), :]))

    def divide(block):
        views = views_t[pl.ds(pl.multiple_of(block * L, L), L), :]
        store_lines(ratio, inner(block * L, L), views / correlate(xcore, lines, block))

    arrive(0)
    divide(3 * planes[0])
    arrive(1)
    for block in (3 * planes[1], 1, 2):
        divide(block)
    for far in (1, 0):
        half = planes[far]
        back = [correlate(xtcore, ratio, 2 * half + k) for k in range(2)]
        send2[half_rows(half), :] = swap_slab(jnp.concatenate(back, axis=0))
        exchange(send2, recv2, 1, far)
    for far in range(2):
        arrived(recv2, 1, far)
        part_ = dot3(ytb, split(recv2[half_rows(planes[far]), :]), NT)
        for k, value in enumerate(split(part_)):
            turned[k, planes[far]] = value

    def quarter(c, b):
        return pl.ds(pl.multiple_of((c * CHIPS + b) * YDIM, YDIM), YDIM)

    def remote(src, dst, sems, index, device):
        send = pltpu.make_async_remote_copy(
            src_ref=src,
            dst_ref=dst,
            send_sem=sems[0].at[index],
            recv_sem=sems[1].at[index],
            device_id=device,
            device_id_type=MESH,
        )
        send.start()
        return send

    order = chips + [chip]
    same_core = [(b * 2 + core, q) for b in chips]
    bh, bl = (jnp.concatenate([turned[k, 0], turned[k, 1]], axis=1) for k in range(2))
    halves = {}
    for half, rows_, window in HALVES:
        corr[0, :, half * 2 * L : (half + 1) * 2 * L] = dot3(
            (bh[:, window], bl[:, window]), (zcol[0, rows_, :], zcol[1, rows_, :]), NN
        )
    for c in range(CHUNKS):
        for k, b in enumerate(order):
            halves[c, k] = remote(
                corr.at[c, quarter(1 - core, b), :], pair.at[c, b],
                (pair_ssem, pair_rsem), c * CHIPS + k, partner,
            )
    quarters = {}
    for c in range(CHUNKS):
        for k, b in enumerate(order):
            halves[c, k].wait_recv()
            pair[c, b] = pair[c, b] * corr[c, quarter(core, b), :]
            if k < CHIPS - 1:
                quarters[c, k] = remote(
                    pair.at[c, b], part.at[c, k],
                    (part_ssem, part_rsem), c * CHIPS + k, same_core[k],
                )
    gathers, locals_, relays = {}, [], []
    mine = quarter(core, chip)
    for c in range(CHUNKS):
        cols = pl.ds(c * HALF, HALF)
        for k in range(CHIPS - 1):
            quarters[c, k].wait_recv()
        own = est_ref[mine, c * HALF : (c + 1) * HALF] * pair[c, chip]
        final[c] = (own * part[c, 0]) * (part[c, 1] * part[c, 2])
        target = out_ref.at[mine, cols]
        for k in range(CHIPS - 1):
            gathers[c, k] = remote(
                final.at[c], target, (chip_ssem, chip_rsem), c * CHIPS + k, same_core[k]
            )
        relays.append(
            remote(final.at[c], target, (core_ssem, core_rsem), c * CHIPS + CHIPS - 1, partner)
        )
        local = pltpu.make_async_copy(final.at[c], target, isem.at[c])
        local.start()
        locals_.append(local)
    for c in range(CHUNKS):
        for k in (2, 1, 0):
            gathers[c, k].wait_recv()
            where = out_ref.at[quarter(core, chips[k]), pl.ds(c * HALF, HALF)]
            relays.append(remote(where, where, (core_ssem, core_rsem), c * CHIPS + k, partner))
    sent(send1, 0)
    sent(send2, 1)
    for sends in (halves, quarters, gathers):
        for send in sends.values():
            send.wait_send()
    for send in relays + locals_:
        send.wait()


def per_device(estimate, views_data, psf_long, psf_short, detection):
    raw = pl.BlockSpec(memory_space=pl.ANY)
    dma = pltpu.SemaphoreType.DMA
    updated = pl.pallas_call(
        kernel,
        out_shape=jax.ShapeDtypeStruct((L, N), F32),
        in_specs=[raw] * 5,
        out_specs=raw,
        scratch_shapes=[
            pltpu.VMEM((L, N), F32),
            pltpu.VMEM((L, N), F32),
            pltpu.VMEM(psf_long.shape, F32),
            pltpu.VMEM(psf_short.shape, F32),
            pltpu.SMEM(detection.shape, jnp.int32),
            pltpu.VMEM((8, L), F32),
            pltpu.VMEM((2, 2 * L, 4 * L), BF16),
            pltpu.VMEM((2, 4 * L, 2 * L), BF16),
            pltpu.VMEM((2 * L, 2 * L), BF16),
            pltpu.VMEM((2 * L, 2 * L), BF16),
            pltpu.VMEM((N, L), F32),
            pltpu.VMEM((N, L), F32),
            pltpu.VMEM((N, L), F32),
            pltpu.VMEM((N, L), F32),
            pltpu.VMEM((N, L), F32),
            pltpu.VMEM((N + 2 * EDGE, 2 * L), BF16),
            pltpu.VMEM((N + 2 * EDGE, 2 * L), BF16),
            pltpu.VMEM((2, 2, L, 2 * L), BF16),
            pltpu.VMEM((CHUNKS, L, HALF), F32),
            pltpu.VMEM((CHUNKS, CHIPS, YDIM, HALF), F32),
            pltpu.VMEM((CHUNKS, CHIPS - 1, YDIM, HALF), F32),
            pltpu.VMEM((CHUNKS, YDIM, HALF), F32),
            dma((5,)), dma((4,)), dma((4,)),
            *[dma((CHUNKS * CHIPS,))] * 8,
        ],
        compiler_params=pltpu.CompilerParams(
            collective_id=0, has_side_effects=True, vmem_limit_bytes=32 << 20
        ),
    )(
        *(
            pltpu.with_memory_space_constraint(a, pltpu.HBM)
            for a in (
                estimate.reshape(L, N),
                views_data.reshape(L, N),
                psf_long,
                psf_short,
                detection,
            )
        )
    )
    return updated.reshape(estimate.shape)


def solution(mesh):
    return jax.shard_map(
        per_device,
        mesh=mesh,
        in_specs=(
            P("pencil", None, None),
            P("view", "pencil", None, None),
            P("view", None),
            P("view", None, None),
            P("view", None),
        ),
        out_specs=P("pencil", None, None),
        check_vma=False,
    )
```
